256 devices in a mesh: leaf: 4 (over y), row: 16 (over z, core), col: 4 (over x).
Axes of the slice: x: 4, y: 4, z: 8, core: 2. Of those that a mesh axis runs over, the one named last changes fastest.
Arguments:
- anc_inverse: float32 [24, 24, 512, 512], P('leaf', None, 'row', 'col'), may hold values from -6 to 6, as said below
- struct_one: int32 [12, 5], P('leaf'), may hold values from 0 to 23, as said below
- lower_one: float32 [12, 5, 512, 512], P('leaf', None, 'row', 'col'), may hold values from -0.125 to 0.125
- pivot_inv_one: float32 [12, 512, 512], P('leaf', 'row', 'col'), may hold values from -6 to 6, as said below
- lower_two: float32 [24, 6, 512, 512], P('leaf', None, 'row', 'col'), may hold values from -0.109375 to 0.109375
- pivot_inv_two: float32 [24, 512, 512], P('leaf', 'row', 'col'), may hold values from -6 to 6, as said below
Outputs:
- offdiag_one: float32 [12, 5, 512, 512], P('leaf', None, 'row', 'col')
- diag_one: float32 [12, 512, 512], P('leaf', 'row', 'col')
- offdiag_two: float32 [24, 6, 512, 512], P('leaf', None, 'row', 'col')
- diag_two: float32 [24, 512, 512], P('leaf', 'row', 'col')
The draws below stay inside these ranges and needn't reach their ends.
Inputs may be any that keep to these rules, and one draw needn't show every extreme that they name: `struct_one`: each row lists 5 different separator block numbers in increasing order. symmetric: anc_inverse[b, a] is the transpose of anc_inverse[a, b]. `pivot_inv_one`: every block equals its transpose. `pivot_inv_two`: every block equals its transpose.
All inputs are finite; a program needn't handle non-finite values.
Results may differ from the reference program's by a relative error of at most 0.0001.
Values sent between devices are 32-bit elements; how exact they have to be, the bound alone decides.
A program may use at most 64 MiB of HBM per device.

```python
import jax
import jax.numpy as jnp
from jax import lax

W = 512
NA = 24
SK1 = 5
K2 = 2
NODES1 = 12
NODES2 = 24


def draw_struct_one(key, part):
    row_keys = jax.random.split(jax.random.fold_in(key, 17), NODES1)

    def one_row(row_key):
        return jax.random.permutation(row_key, NA)
    shuffled = jax.vmap(one_row)(row_keys)
    return jnp.sort(shuffled[:, :SK1], axis=1).astype(jnp.int32)


def raw_values(key, shape):
    return jax.random.normal(key, shape, jnp.float32)


def draw_anc_inverse(key, part):
    values = raw_values(jax.random.fold_in(key, 31), (NA, NA, W, W))
    both = (values + jnp.transpose(values, (1, 0, 3, 2))) * 0.70710678
    return jnp.clip(both, -6.0, 6.0)


def symmetric_pivots(key, count):
    values = raw_values(key, (count, W, W))
    both = (values + jnp.transpose(values, (0, 2, 1))) * 0.70710678
    return jnp.clip(both, -6.0, 6.0)


def draw_pivot_inv_one(key, part):
    return symmetric_pivots(jax.random.fold_in(key, 41), NODES1)


def draw_pivot_inv_two(key, part):
    return symmetric_pivots(jax.random.fold_in(key, 43), NODES2)


def block_levels(own_key, shape, pieces, low, top_value):
    level, own = 1.0, jax.random.fold_in(own_key, 6)
    for axis_at, shards_of in pieces:
        steps = jnp.exp(jax.random.uniform(jax.random.fold_in(own, axis_at), (shards_of,), jnp.float32, low / len(pieces), top_value / len(pieces)))
        level = level * jnp.repeat(steps, shape[axis_at] // shards_of).reshape([-1 if axis == axis_at else 1 for axis in range(len(shape))])
    return level


def gaussian(key, shape, scale, bound, cuts=(), kind=jnp.bfloat16):
    values = jax.random.normal(key, shape, jnp.float32) * scale
    if len(cuts) > 0:
        values = block_levels(key, shape, cuts, -0.22, 0.18) * values
    return jnp.clip(values, min=-bound, max=bound).astype(kind)


def setup_inputs(seed: int = 0) -> dict:
    seeds = jax.random.split(jax.random.key(seed), 7)
    return {
        "anc_inverse": draw_anc_inverse(jax.random.fold_in(seeds[6], 71), 0),
        "struct_one": draw_struct_one(jax.random.fold_in(seeds[6], 71), 0),
        "lower_one": gaussian(seeds[2], (NODES1, SK1, W, W), (SK1 * W) ** -0.5, 0.125, ((0, 4), (2, 16), (3, 4)), jnp.float32),
        "pivot_inv_one": draw_pivot_inv_one(jax.random.fold_in(seeds[6], 71), 0),
        "lower_two": gaussian(seeds[4], (NODES2, SK1 + 1, W, W), ((SK1 + 1) * W) ** -0.5, 0.109375, ((0, 4), (2, 16), (3, 4)), jnp.float32),
        "pivot_inv_two": draw_pivot_inv_two(jax.random.fold_in(seeds[6], 71), 0),
    }


highest = lax.Precision.HIGHEST


def reference(anc_inverse, struct_one, lower_one, pivot_inv_one, lower_two, pivot_inv_two):
    outs_one = []
    diags_one = []
    outs_two = []
    diags_two = []
    for supernode in range(NODES1):
        listed = struct_one[supernode].astype(jnp.int32)
        picked = anc_inverse[listed[:, None], listed[None, :]]
        offdiag = -jnp.einsum("stik,tkj->sij", picked, lower_one[supernode], precision=highest)
        diagonal = pivot_inv_one[supernode] - jnp.einsum("ski,skj->ij", lower_one[supernode], offdiag, precision=highest)
        outs_one.append(offdiag)
        diags_one.append(diagonal)
        upper_rows = jnp.concatenate([picked, offdiag[:, None]], axis=1)
        last_row = jnp.concatenate([jnp.swapaxes(offdiag, 1, 2), diagonal[None]], axis=0)[None]
        known_inverse = jnp.concatenate([upper_rows, last_row], axis=0)
        for child in range(K2):
            factor = lower_two[supernode * K2 + child]
            offdiag_child = -jnp.einsum("pqik,qkj->pij", known_inverse, factor, precision=highest)
            diag_child = pivot_inv_two[supernode * K2 + child] - jnp.einsum("pki,pkj->ij", factor, offdiag_child, precision=highest)
            outs_two.append(offdiag_child)
            diags_two.append(diag_child)
    return jnp.stack(outs_one), jnp.stack(diags_one), jnp.stack(outs_two), jnp.stack(diags_two)
```

```python
import jax
import jax.numpy as jnp
from jax import lax
from jax.experimental import pallas as pl
from jax.experimental.pallas import tpu as pltpu
from jax.sharding import PartitionSpec as P

F32 = jnp.float32
BF16 = jnp.bfloat16
MESH = pl.DeviceIdType.MESH
TR = 32
TC = 128
NM = 3
SK = 5
NC = 2
NJ = NM * NC
NL = NM * SK
NA2 = NJ * SK
NX = 4
NY = 4
NZ = 8
NR = 2 * NZ
LEAF_BLOCKS = 6
BLK = SK * SK
YH = 13
B1 = NL + NJ
XB1 = B1 + NM
GT = 5 * NM
GA = 8
N_COPIES = 4 + 4 + 4 * NM + 6 * NM + 2 * (8 + 8) + 1 + 8


def split(a):
    hi = a.astype(BF16)
    return hi, (a - hi.astype(F32)).astype(BF16)


def dot3(a, b, lhs_dim):
    ah, al = split(a)
    bh, bl = split(b)

    def one(u, v):
        return lax.dot_general(
            u, v, (((lhs_dim,), (0,)), ((), ())), preferred_element_type=F32
        )

    return one(ah, bh) + (one(ah, bl) + one(al, bh))


def kernel(
    st, g, low1, piv1, low2, piv2,
    off1, diag1, off2, diag2,
    xb1, xb2, x3, zb1, zb2, ysel, yo, yl, yr,
    zacc, pb, gp, sr, send_r, send_l, in_r, in_l,
    ssem, rsem,
):
    y = lax.axis_index("leaf")
    r = lax.axis_index("row")
    x = lax.axis_index("col")
    z = r // 2
    h = r % 2

    def wrap(v, n):
        return lax.rem(v + n, n)

    def dev(yy, rr, xx):
        return (yy, rr, xx)

    def zrow(zz):
        return 2 * wrap(zz, NZ) + h

    x_right, x_left = dev(y, r, wrap(x + 1, NX)), dev(y, r, wrap(x - 1, NX))
    y_right, y_left = dev(wrap(y + 1, NY), r, x), dev(wrap(y - 1, NY), r, x)
    z_right, z_left = dev(y, zrow(z + 1), x), dev(y, zrow(z - 1), x)
    sibling = dev(y, 2 * z + 1 - h, x)

    copies = []

    def send(src, dst, to):
        k = len(copies)
        c = pltpu.make_async_remote_copy(
            src_ref=src, dst_ref=dst, send_sem=ssem.at[k], recv_sem=rsem.at[k],
            device_id=to, device_id_type=MESH,
        )
        c.start()
        copies.append(c)
        return c

    barrier = pltpu.get_barrier_semaphore()
    partners = (x_right, x_left, y_right, y_left, z_right, z_left, sibling)
    for d in partners:
        pl.semaphore_signal(barrier, inc=1, device_id=d, device_id_type=MESH)
    pl.semaphore_wait(barrier, len(partners))

    def x_first(buf):
        own = buf.at[x]
        return send(own, own, x_right), send(own, own, x_left)

    def x_second(buf, first, n):
        half = n // 2
        first[0].wait_recv()
        a = buf.at[wrap(x - 1, NX), pl.ds(0, half)]
        fa = send(a, a, x_right)
        first[1].wait_recv()
        b = buf.at[wrap(x + 1, NX), pl.ds(half, n - half)]
        return fa, send(b, b, x_left)

    def z_start(buf):
        own = buf.at[r]
        return dict(
            buf=buf,
            right=send(own, own, z_right),
            left=send(own, own, z_left),
            sib=[send(own, own, sibling)],
        )

    def z_step(s, step, n):
        half = n // 2
        buf = s["buf"]
        last = step == 3
        right, left = s["right"], s["left"]
        right.wait_recv()
        a = buf.at[zrow(z - step)]
        ap = buf.at[zrow(z - step), pl.ds(0, half)] if last else a
        s["right"] = send(ap, ap, z_right)
        s["sib"].append(send(a, a, sibling))
        left.wait_recv()
        b = buf.at[zrow(z + step)]
        bp = buf.at[zrow(z + step), pl.ds(half, n - half)] if last else b
        s["left"] = send(bp, bp, z_left)
        s["sib"].append(send(b, b, sibling))

    def z_finish(s):
        s["right"].wait_recv()
        s["left"].wait_recv()
        far = s["buf"].at[zrow(z + 4)]
        s["sib"].append(send(far, far, sibling))
        for c in s["sib"]:
            c.wait_recv()

    xb1[x, 0:NL] = low1[...].reshape(NL, TR, TC)
    zb1[r, 0:NL] = low1[...].reshape(NL, TR, TC)
    for j in range(NJ):
        xb1[x, NL + j] = low2[j, SK]
        zb1[r, NL + j] = low2[j, SK]
    xb1[x, B1:XB1] = piv1[...]
    z1 = z_start(zb1)
    xf1 = x_first(xb1)

    def select(delta, m):
        base = (wrap(y + delta, NY) * NM + m) * SK

        def row(q, carry):
            sq = st[base + q]
            for p in range(SK):
                sp = st[base + p]
                mine = sp // LEAF_BLOCKS == y
                a = jnp.clip(sp - y * LEAF_BLOCKS, 0, LEAF_BLOCKS - 1)
                tile = g[a, sq]
                ysel[delta, m, q * SK + p] = jnp.where(mine, tile, jnp.zeros_like(tile))
            return carry

        lax.fori_loop(0, SK, row, 0)

    lo, hi = pl.ds(0, YH), pl.ds(YH, BLK - YH)
    opp = []
    for m in range(NM):
        select(2, m)
        opp.append(
            (
                send(ysel.at[2, m, lo], yo.at[m, lo], y_right),
                send(ysel.at[2, m, hi], yo.at[m, hi], y_left),
            )
        )
    direct = []
    for m in range(NM):
        select(1, m)
        c = send(ysel.at[1, m, hi], yl.at[m, hi], y_right)
        select(3, m)
        direct.append((c, send(ysel.at[3, m, lo], yr.at[m, lo], y_left)))

    merged = []

    def merge(m):
        opp[m][0].wait_recv()
        ysel[1, m, 0:YH] = ysel[1, m, 0:YH] + yo[m, 0:YH]
        c = send(ysel.at[1, m, lo], yl.at[m, lo], y_right)
        opp[m][1].wait_recv()
        ysel[3, m, YH:BLK] = ysel[3, m, YH:BLK] + yo[m, YH:BLK]
        merged.append((c, send(ysel.at[3, m, hi], yr.at[m, hi], y_left)))

    z_step(z1, 1, B1)
    for m in range(NM):
        select(0, m)
    merge(0)
    xs1 = x_second(xb1, xf1, XB1)
    z_step(z1, 2, B1)
    merge(1)
    z_step(z1, 3, B1)
    merge(2)
    for c in xs1:
        c.wait_recv()
    z_finish(z1)

    def stack(buf, first, count):
        return jnp.concatenate(
            [
                buf[c, pl.ds(first, count)].reshape(count * TR, TC)
                for c in range(NX)
            ],
            axis=1,
        )

    def rows_of(buf, i):
        return buf[:, i].reshape(NR * TR, TC)

    def correct(m, carry):
        lhs = jnp.concatenate([stack(xb1, m * SK, SK), stack(xb1, B1 + m, 1)], axis=0)
        rhs = jnp.concatenate(
            [rows_of(zb1, NL + m * NC + c) for c in range(NC)], axis=1
        )
        prod = dot3(lhs, rhs, 1)
        for c in range(NC):
            j = m * NC + c
            part = prod[:, c * TC : (c + 1) * TC]
            fixed = low2[j, 0:SK] - part[: SK * TR].reshape(SK, TR, TC)
            xb2[x, pl.ds(j * SK, SK)] = fixed
            zb2[r, pl.ds(j * SK, SK)] = fixed
            pb[j] = part[SK * TR :]
        return carry

    lax.fori_loop(0, NM, correct, 0)
    z2 = z_start(zb2)
    xf2 = x_first(xb2)

    xf3, xs3 = [], []

    def own_stripe(m):
        for c in direct[m] + merged[m]:
            c.wait_recv()
        x3[x, m] = ysel[0, m] + yl[m] + yr[m]
        own = x3.at[x, m]
        xf3.append((send(own, own, x_right), send(own, own, x_left)))

    def pass_stripe(m):
        half = YH
        xf3[m][0].wait_recv()
        a = x3.at[wrap(x - 1, NX), m, pl.ds(0, half)]
        fa = send(a, a, x_right)
        xf3[m][1].wait_recv()
        b = x3.at[wrap(x + 1, NX), m, pl.ds(half, BLK - half)]
        xs3.append((fa, send(b, b, x_left)))

    own_stripe(0)
    own_stripe(1)
    xs2 = x_second(xb2, xf2, NA2)
    z_step(z2, 1, NA2)
    own_stripe(2)
    pass_stripe(0)
    z_step(z2, 2, NA2)
    pass_stripe(1)
    z_step(z2, 3, NA2)
    pass_stripe(2)
    for c in xs2:
        c.wait_recv()
    z_finish(z2)

    for m in range(NM):
        for c in xs3[m]:
            c.wait_recv()
        zacc[...] = jnp.zeros_like(zacc)

        def block(q, carry, m=m):
            lhs = jnp.concatenate(
                [
                    x3[c, m, pl.ds(q * SK, SK)].reshape(SK * TR, TC)
                    for c in range(NX)
                ],
                axis=1,
            )
            rhs = jnp.concatenate(
                [rows_of(zb1, m * SK + q)]
                + [rows_of(zb2, (m * NC + c) * SK + q) for c in range(NC)],
                axis=1,
            )
            zacc[...] += dot3(lhs, rhs, 1)
            return carry

        lax.fori_loop(0, SK, block, 0)
        off1[m] = -zacc[:, 0:TC].reshape(SK, TR, TC)
        for c in range(NC):
            off2[m * NC + c, 0:SK] = -zacc[:, (c + 1) * TC : (c + 2) * TC].reshape(
                SK, TR, TC
            )
        left = dot3(stack(xb1, m * SK, SK), zacc[...], 0)
        parts = [left[:, b * TC : (b + 1) * TC] for b in range(1 + NC)]
        for c in range(NC):
            j = m * NC + c
            lhs = jnp.concatenate(
                [stack(xb2, j * SK, SK), stack(xb1, NL + j, 1)], axis=0
            )
            rhs = jnp.concatenate(
                [zacc[:, (c + 1) * TC : (c + 2) * TC], pb[j]], axis=0
            )
            parts.append(dot3(lhs, rhs, 0))
        for b in range(5):
            tiles = parts[b].reshape(NZ, 2, TR, TC)
            for hh in range(2):
                gp[hh, :, m * 5 + b] = tiles[:, hh]

    cs = send(gp.at[1 - h], sr, sibling)
    cs.wait_recv()

    def mine(zz, a, b):
        zz = wrap(zz, NZ)
        return gp[h, zz, a:b] + sr[zz, a:b]

    send_r[0, 0:GA] = mine(z + 4, 0, GA)
    a = pl.ds(0, GA)
    cr = send(send_r.at[0, a], in_r.at[0, a], z_right)
    send_l[0, GA:GT] = mine(z - 4, GA, GT)
    b = pl.ds(GA, GT - GA)
    cl = send(send_l.at[0, b], in_l.at[0, b], z_left)
    for s in range(1, 4):
        cr.wait_recv()
        if s == 1:
            send_r[1, 0:GA] = in_r[0, 0:GA] + mine(z + 3, 0, GA)
            send_r[1, GA:GT] = mine(z + 3, GA, GT)
        else:
            send_r[s] = in_r[s - 1] + mine(z + 4 - s, 0, GT)
        cr = send(send_r.at[s], in_r.at[s], z_right)
        cl.wait_recv()
        if s == 1:
            send_l[1, 0:GA] = mine(z - 3, 0, GA)
            send_l[1, GA:GT] = in_l[0, GA:GT] + mine(z - 3, GA, GT)
        else:
            send_l[s] = in_l[s - 1] + mine(z - 4 + s, 0, GT)
        cl = send(send_l.at[s], in_l.at[s], z_left)
    cr.wait_recv()
    cl.wait_recv()
    total = in_r[3] + in_l[3] + mine(z, 0, GT)
    for m in range(NM):
        diag1[m] = piv1[m] + total[m * 5]
        for c in range(NC):
            j = m * NC + c
            off2[j, SK] = total[m * 5 + 1 + c] - pb[j]
            diag2[j] = piv2[j] + total[m * 5 + 3 + c]
    assert len(copies) == N_COPIES, len(copies)
    for c in copies:
        c.wait_send()


def on_device(anc_inverse, struct_one, lower_one, pivot_inv_one, lower_two, pivot_inv_two):
    listed = lax.all_gather(struct_one, "leaf", axis=0, tiled=True).reshape(-1)
    tile = (TR, TC)

    def like(*lead):
        return jax.ShapeDtypeStruct(lead + tile, F32)

    def vmem(*lead):
        return pltpu.VMEM(lead + tile, F32)

    whole = pl.BlockSpec(memory_space=pltpu.VMEM)
    return pl.pallas_call(
        kernel,
        out_shape=(like(NM, SK), like(NM), like(NJ, SK + 1), like(NJ)),
        in_specs=[pl.BlockSpec(memory_space=pltpu.SMEM)] + [whole] * 5,
        out_specs=(whole,) * 4,
        scratch_shapes=[
            vmem(NX, XB1),
            vmem(NX, NA2),
            vmem(NX, NM, BLK),
            vmem(NR, B1),
            vmem(NR, NA2),
            vmem(NY, NM, BLK),
            vmem(NM, BLK),
            vmem(NM, BLK),
            vmem(NM, BLK),
            pltpu.VMEM((SK * TR, (1 + NC) * TC), F32),
            vmem(NJ),
            vmem(2, NZ, GT),
            vmem(NZ, GT),
            vmem(4, GT),
            vmem(4, GT),
            vmem(4, GT),
            vmem(4, GT),
            pltpu.SemaphoreType.DMA((N_COPIES,)),
            pltpu.SemaphoreType.DMA((N_COPIES,)),
        ],
        compiler_params=pltpu.CompilerParams(
            collective_id=0, has_side_effects=True, vmem_limit_bytes=60 * 2**20
        ),
    )(listed, anc_inverse, lower_one, pivot_inv_one, lower_two, pivot_inv_two)


def solution(mesh):
    placed = (
        P("leaf", None, "row", "col"),
        P("leaf", None),
        P("leaf", None, "row", "col"),
        P("leaf", "row", "col"),
        P("leaf", None, "row", "col"),
        P("leaf", "row", "col"),
    )
    return jax.shard_map(
        on_device,
        mesh=mesh,
        in_specs=placed,
        out_specs=(
            P("leaf", None, "row", "col"),
            P("leaf", "row", "col"),
            P("leaf", None, "row", "col"),
            P("leaf", "row", "col"),
        ),
        check_vma=False,
    )
```

```python
import jax
import jax.numpy as jnp
from jax import lax
from jax.experimental import pallas as pl
from jax.experimental.pallas import tpu as pltpu
from jax.sharding import PartitionSpec as P

F32 = jnp.float32
BF16 = jnp.bfloat16
I32 = jnp.int32
MESH = pl.DeviceIdType.MESH
TR = 32
TC = 128
NM = 3
SK = 5
NC = 2
NJ = NM * NC
NL = NM * SK
NX = 4
NY = 4
NZ = 8
NR = 2 * NZ
NA_LEAF = 6
NA_ALL = 24
BLK = SK * SK
UNITS = ((0, 13), (13, 12))
HALF = (7, 6)
GT = 3
N_OUT = 42
N_IN = 220
N_LOADS = 8
N_STORES = NM + NJ + 3


def split(a):
    hi = a.astype(BF16)
    return hi, (a - hi.astype(F32)).astype(BF16)


def dot3(a, b, lhs_dim):
    ah, al = split(a)
    bh, bl = split(b)

    def one(u, v):
        return lax.dot_general(
            u, v, (((lhs_dim,), (0,)), ((), ())), preferred_element_type=F32
        )

    return one(ah, bh) + (one(ah, bl) + one(al, bh))


def kernel(
    st, g_in, low1, piv1, low2, piv2,
    off1_out, diag1_out, off2_out, diag2_out,
    off1, diag1, off2, diag2,
    gv, av, p2, sv, xl, xb, xa, x3, zb, zl, za, ysel, yo, yn,
    zacc0, zacc1, pb, gp, sr, send_r, send_l, in_r, in_l,
    sm, ssem, rsem, lsem, msem, osem,
):
    y = lax.axis_index("leaf")
    r = lax.axis_index("row")
    x = lax.axis_index("col")
    z = r // 2
    h = r % 2

    def wrap(v, n):
        return lax.rem(v + n, n)

    def zrow(zz):
        return 2 * wrap(zz, NZ) + h

    x_right, x_left = (y, r, wrap(x + 1, NX)), (y, r, wrap(x - 1, NX))
    y_right, y_left = (wrap(y + 1, NY), r, x), (wrap(y - 1, NY), r, x)
    y_far = (wrap(y + 2, NY), r, x)
    z_right, z_left = (y, zrow(z + 1), x), (y, zrow(z - 1), x)
    sibling = (y, 2 * z + 1 - h, x)

    outs, ins, drains = [], [], []

    def next_out(sent):
        sem = ssem.at[len(outs)]
        outs.append(sem)
        drains.append((sent, sem))
        return sem

    def next_in():
        sem = rsem.at[len(ins)]
        ins.append(sem)
        return sem

    def take(ref, sem):
        pltpu.make_async_copy(ref, ref, sem).wait()

    def send(src, dst, to, out, into):
        c = pltpu.make_async_remote_copy(
            src_ref=src, dst_ref=dst, send_sem=out, recv_sem=into,
            device_id=to, device_id_type=MESH,
        )
        c.start()
        return c

    loads = [
        (low2.at[:, SK], zb.at[r]),
        (low1, xl.at[x, pl.ds(0, NL)]),
        (piv1, xl.at[x, pl.ds(NL, NM)]),
        (low1, zl.at[r]),
        (low2.at[:, SK], xb.at[x]),
        (g_in, gv),
        (low2.at[:, pl.ds(0, SK)], av),
        (piv2, p2),
    ]
    loads = [pltpu.make_async_copy(a, b, lsem.at[i]) for i, (a, b) in enumerate(loads)]
    for c in loads:
        c.start()
    lane = lax.broadcasted_iota(I32, (8, TC), 1)
    listed = jnp.zeros((8, TC), I32)
    for m in range(NM):
        for p in range(SK):
            listed = jnp.where(lane == m * SK + p, st[m, p], listed)
    sv[y] = listed

    barrier = pltpu.get_barrier_semaphore()
    partners = (x_right, x_left, y_right, y_left, y_far, z_right, z_left, sibling)
    for d in partners:
        pl.semaphore_signal(barrier, inc=1, device_id=d, device_id_type=MESH)
    pl.semaphore_wait(barrier, len(partners))

    class XRing:
        def __init__(self, at, n, half):
            self.at, self.n, self.half = at, n, half

        def start(self):
            self.out = next_out(self.at(pl.ds(0, 3)))
            own = self.at(x)
            self.a = send(own, own, x_right, self.out, next_in())
            self.b = send(own, own, x_left, self.out, next_in())

        def second(self):
            self.a.wait_recv()
            a = self.at(wrap(x - 1, NX)).at[pl.ds(0, self.half)]
            self.a = send(a, a, x_right, self.out, next_in())
            self.b.wait_recv()
            b = self.at(wrap(x + 1, NX)).at[pl.ds(self.half, self.n - self.half)]
            self.b = send(b, b, x_left, self.out, next_in())

        def finish(self):
            self.a.wait_recv()
            self.b.wait_recv()

    class ZRing:
        def __init__(self, at, n, half):
            self.at, self.n, self.half = at, n, half

        def start(self):
            self.out = next_out(self.at(pl.ds(0, 2 * NZ - 1)))
            self.sib = next_in()
            own = self.at(r)
            self.a = send(own, own, z_right, self.out, next_in())
            self.b = send(own, own, z_left, self.out, next_in())
            send(own, own, sibling, self.out, self.sib)

        def step(self, i):
            self.a.wait_recv()
            a = self.at(zrow(z - i))
            part = a.at[pl.ds(0, self.half)] if i == 3 else a
            self.a = send(part, part, z_right, self.out, next_in())
            self.b.wait_recv()
            b = self.at(zrow(z + i))
            part = b.at[pl.ds(self.half, self.n - self.half)] if i == 3 else b
            self.b = send(part, part, z_left, self.out, next_in())
            send(a, a, sibling, self.out, self.sib)
            send(b, b, sibling, self.out, self.sib)

        def last(self):
            self.a.wait_recv()
            self.b.wait_recv()
            far = self.at(zrow(z + 4))
            send(far, far, sibling, self.out, self.sib)

        def finish(self):
            take(self.at(pl.ds(0, NZ)), self.sib)

    z_b = [
        ZRing(lambda i, m=m: zb.at[i, pl.ds(m * NC, NC)], NC, 1) for m in range(NM)
    ]
    z_l = [
        ZRing(lambda i, m=m: zl.at[i, pl.ds(m * SK, SK)], SK, 2 + m % 2)
        for m in range(NM)
    ]
    z_a = [ZRing(lambda i, j=j: za.at[i, j], SK, 2 + j % 2) for j in range(NJ)]
    x_lp = XRing(lambda i: xl.at[i], NL + NM, (NL + NM) // 2)
    x_b = XRing(lambda i: xb.at[i], NJ, NJ // 2)
    x_a = [XRing(lambda i, m=m: xa.at[i, m], NC * SK, SK) for m in range(NM)]
    x_s = [
        XRing(lambda i, k=k: x3.at[i, k // 2, pl.ds(*UNITS[k % 2])], UNITS[k % 2][1], HALF[k % 2])
        for k in range(2 * NM)
    ]

    listed_in = next_in()

    def send_lists():
        out = next_out(sv.at[pl.ds(0, NY - 1)])
        own = sv.at[y]
        for d in (y_right, y_left, y_far):
            send(own, own, d, out, listed_in)

    def take_lists():
        take(sv.at[pl.ds(0, NY - 1)], listed_in)
        to_scalars = pltpu.make_async_copy(sv, sm, msem)
        to_scalars.start()
        to_scalars.wait()

    def select(delta, k):
        m, (first, count) = k // 2, UNITS[k % 2]
        to = wrap(y + delta, NY)

        def tile_of(e, carry):
            sq = sm[to, 0, m * SK + e // SK]
            sp = sm[to, 0, m * SK + lax.rem(e, SK)]
            mine = sp // NA_LEAF == y
            a = jnp.clip(sp - y * NA_LEAF, 0, NA_LEAF - 1)
            tile = gv[a, sq]
            ysel[delta, m, e] = jnp.where(mine, tile, jnp.zeros_like(tile))
            return carry

        lax.fori_loop(first, first + count, tile_of, 0)

    def halves(k):
        first, count = UNITS[k % 2]
        half = HALF[k % 2]
        return pl.ds(first, half), pl.ds(first + half, count - half)

    y_out = [next_out(ysel.at[pl.ds(0, 3), 0, pl.ds(0, n)]) for _, n in UNITS * NM]
    far_in = [next_in() for _ in range(2 * NM)]
    near_in = [next_in() for _ in range(2 * NM)]

    def y_far_half(k):
        select(2, k)
        m, (lo, hi) = k // 2, halves(k)
        send(ysel.at[2, m, lo], yo.at[m, lo], y_right, y_out[k], far_in[k])
        send(ysel.at[2, m, hi], yo.at[m, hi], y_left, y_out[k], far_in[k])

    def y_near_half(k):
        m, (lo, hi) = k // 2, halves(k)
        select(1, k)
        send(ysel.at[1, m, hi], yn.at[m, 0, hi], y_right, y_out[k], near_in[k])
        select(3, k)
        send(ysel.at[3, m, lo], yn.at[m, 1, lo], y_left, y_out[k], near_in[k])

    def y_merge(k):
        m, (lo, hi) = k // 2, halves(k)
        take(yo.at[m, pl.ds(*UNITS[k % 2])], far_in[k])
        ysel[1, m, lo] = ysel[1, m, lo] + yo[m, lo]
        send(ysel.at[1, m, lo], yn.at[m, 0, lo], y_right, y_out[k], near_in[k])
        ysel[3, m, hi] = ysel[3, m, hi] + yo[m, hi]
        send(ysel.at[3, m, hi], yn.at[m, 1, hi], y_left, y_out[k], near_in[k])

    def y_last(k):
        m, tiles = k // 2, pl.ds(*UNITS[k % 2])
        take(yn.at[m, :, tiles], near_in[k])
        x3[x, m, tiles] = ysel[0, m, tiles] + yn[m, 0, tiles] + yn[m, 1, tiles]
        x_s[k].start()

    def wide(tiles):
        return jnp.concatenate([t.reshape(-1, TC) for t in tiles], axis=1)

    def tall(tiles):
        return tiles.reshape(NR * TR, TC)

    stores = []

    def store(src, dst):
        c = pltpu.make_async_copy(src, dst, osem.at[len(stores)])
        c.start()
        stores.append(c)

    def low_cols(m):
        return wide([xl[i, m * SK : (m + 1) * SK] for i in range(NX)])

    def correct(m):
        lhs = jnp.concatenate(
            [low_cols(m), wide([xl[i, NL + m] for i in range(NX)])], axis=0
        )
        rhs = jnp.concatenate([tall(zb[:, m * NC + c]) for c in range(NC)], axis=1)
        prod = dot3(lhs, rhs, 1)
        for c in range(NC):
            j = m * NC + c
            part = prod[:, c * TC : (c + 1) * TC]
            fixed = av[j] - part[: SK * TR].reshape(SK, TR, TC)
            xa[x, m, c * SK : (c + 1) * SK] = fixed
            za[r, j] = fixed
            pb[j] = part[SK * TR :]

    def multiply(j):
        m, c = j // NC, j % NC
        zacc = zacc1 if c else zacc0
        zacc[...] = jnp.zeros_like(zacc)

        def block(q, carry):
            lhs = wide([x3[i, m, pl.ds(q * SK, SK)] for i in range(NX)])
            rhs = tall(za[:, j, q])
            if c == 0:
                rhs = jnp.concatenate([tall(zl[:, m * SK + q]), rhs], axis=1)
            zacc[...] += dot3(lhs, rhs, 1)
            return carry

        lax.fori_loop(0, SK, block, 0)
        own = zacc[:, (1 - c) * TC : (2 - c) * TC] if c == 0 else zacc[...]
        left = dot3(low_cols(m), zacc[...], 0)
        parts = [left[:, b * TC : (b + 1) * TC] for b in range(2 - c)]
        lhs = jnp.concatenate(
            [
                wide([xa[i, m, c * SK : (c + 1) * SK] for i in range(NX)]),
                wide([xb[i, j] for i in range(NX)]),
            ],
            axis=0,
        )
        parts.append(dot3(lhs, jnp.concatenate([own, pb[j]], axis=0), 0))
        for b, part in enumerate(parts):
            tiles = part.reshape(NZ, 2, TR, TC)
            for hh in range(2):
                gp[hh, j, :, b] = tiles[:, hh]
        reduces[j].share()
        off2[j, 0:SK] = -own.reshape(SK, TR, TC)
        upper = pl.ds(0, SK)
        store(off2.at[j, upper], off2_out.at[j, upper])
        if c == 0:
            off1[m] = -zacc[:, 0:TC].reshape(SK, TR, TC)
            store(off1.at[m], off1_out.at[m])

    class Reduce:
        def __init__(self, j):
            self.j, self.m, self.c = j, j // NC, j % NC
            self.n = 3 - self.c
            self.half = 1 if self.c or self.m % 2 else 2

        def mine(self, zz, a=0, b=None):
            zz = wrap(zz, NZ)
            b = self.n if b is None else b
            return gp[h, self.j, zz, a:b] + sr[self.j, zz, a:b]

        def share(self):
            part = pl.ds(0, self.n)
            out = next_out(gp.at[0, self.j, :, part])
            self.s = send(
                gp.at[1 - h, self.j, :, part],
                sr.at[self.j, :, part],
                sibling,
                out,
                next_in(),
            )

        def start(self):
            j, n, k = self.j, self.n, self.half
            self.out = next_out(gp.at[0, j, pl.ds(0, NZ - 1), pl.ds(0, n)])
            self.s.wait_recv()
            a, b = pl.ds(0, k), pl.ds(k, n - k)
            send_r[j, 0, 0:k] = self.mine(z + 4, 0, k)
            self.a = send(
                send_r.at[j, 0, a], in_r.at[j, 0, a], z_right, self.out, next_in()
            )
            send_l[j, 0, k:n] = self.mine(z - 4, k, n)
            self.b = send(
                send_l.at[j, 0, b], in_l.at[j, 0, b], z_left, self.out, next_in()
            )

        def step(self, s):
            j, n, k = self.j, self.n, self.half
            every = pl.ds(0, n)
            self.a.wait_recv()
            if s == 1:
                send_r[j, 1, 0:k] = in_r[j, 0, 0:k] + self.mine(z + 3, 0, k)
                send_r[j, 1, k:n] = self.mine(z + 3, k, n)
            else:
                send_r[j, s, 0:n] = in_r[j, s - 1, 0:n] + self.mine(z + 4 - s)
            self.a = send(
                send_r.at[j, s, every], in_r.at[j, s, every], z_right, self.out, next_in()
            )
            self.b.wait_recv()
            if s == 1:
                send_l[j, 1, 0:k] = self.mine(z - 3, 0, k)
                send_l[j, 1, k:n] = in_l[j, 0, k:n] + self.mine(z - 3, k, n)
            else:
                send_l[j, s, 0:n] = in_l[j, s - 1, 0:n] + self.mine(z - 4 + s)
            self.b = send(
                send_l.at[j, s, every], in_l.at[j, s, every], z_left, self.out, next_in()
            )

        def finish(self):
            j, m, c, n = self.j, self.m, self.c, self.n
            self.a.wait_recv()
            self.b.wait_recv()
            total = in_r[j, 3, 0:n] + in_l[j, 3, 0:n] + self.mine(z)
            if c == 0:
                diag1[m] = xl[x, NL + m] + total[0]
            off2[j, SK] = total[n - 2] - pb[j]
            diag2[j] = p2[j] + total[n - 1]

    reduces = [Reduce(j) for j in range(NJ)]

    for c in loads:
        c.wait()

    x_lp.start()
    z_b[0].start()
    send_lists()
    z_l[0].start()
    z_b[1].start()
    z_b[2].start()
    z_b[0].step(1)
    x_b.start()
    take_lists()
    y_far_half(0)
    select(0, 0)
    select(0, 3)
    y_near_half(0)
    z_b[1].step(1)
    z_b[2].step(1)
    z_b[0].step(2)
    select(0, 2)
    select(0, 5)
    z_l[0].step(1)
    select(0, 4)
    x_lp.second()
    z_b[1].step(2)
    y_merge(0)
    y_far_half(1)
    y_near_half(1)
    z_b[0].step(3)
    z_l[1].start()
    z_l[2].start()
    x_b.second()
    z_l[0].step(2)
    z_b[1].step(3)
    z_b[2].step(2)
    z_b[0].last()
    y_last(0)
    z_b[0].finish()
    z_l[1].step(1)
    x_lp.finish()
    x_b.finish()
    correct(0)
    z_a[0].start()
    z_a[1].start()
    y_merge(1)
    y_far_half(2)
    select(0, 1)
    y_near_half(2)
    x_a[0].start()
    z_l[0].step(3)
    z_b[1].last()
    z_b[2].step(3)
    z_b[1].finish()
    correct(1)
    x_a[1].start()
    z_a[3].start()
    z_l[1].step(2)
    y_last(1)
    x_s[0].second()
    z_a[2].start()
    z_l[2].step(1)
    z_a[0].step(1)
    y_merge(2)
    y_far_half(3)
    y_near_half(3)
    z_a[1].step(1)
    x_a[0].second()
    z_b[2].last()
    z_b[2].finish()
    correct(2)
    x_a[2].start()
    z_a[5].start()
    z_a[3].step(1)
    z_l[0].last()
    x_a[1].second()
    z_l[0].finish()
    z_l[1].step(3)
    y_last(2)
    z_a[4].start()
    z_a[2].step(1)
    y_merge(3)
    y_far_half(4)
    y_near_half(4)
    x_s[1].second()
    z_l[2].step(2)
    z_a[0].step(2)
    x_s[0].finish()
    z_a[1].step(2)
    x_a[0].finish()
    z_a[5].step(1)
    y_last(3)
    y_merge(4)
    y_far_half(5)
    y_near_half(5)
    z_a[3].step(2)
    z_l[1].last()
    x_a[2].second()
    x_a[1].finish()
    z_l[1].finish()
    z_a[4].step(1)
    y_last(4)
    z_l[2].step(3)
    y_merge(5)
    z_a[0].step(3)
    x_s[1].finish()
    z_a[1].step(3)
    y_last(5)
    z_a[5].step(2)
    z_a[3].step(3)
    z_a[4].step(2)
    z_a[2].step(2)
    z_l[2].last()
    z_a[0].last()
    x_a[2].finish()
    z_a[1].last()
    z_a[0].finish()
    multiply(0)
    z_a[1].finish()
    x_s[4].second()
    multiply(1)
    reduces[0].start()
    z_a[3].last()
    z_l[2].finish()
    x_s[2].second()
    z_a[4].step(3)
    z_a[3].finish()
    reduces[1].start()
    z_a[5].step(3)
    x_s[5].second()
    reduces[0].step(1)
    z_a[2].step(3)
    x_s[3].second()
    z_a[4].last()
    x_s[4].finish()
    z_a[5].last()
    z_a[4].finish()
    reduces[1].step(1)
    z_a[5].finish()
    reduces[0].step(2)
    x_s[2].finish()
    z_a[2].last()
    z_a[2].finish()
    reduces[1].step(2)
    x_s[5].finish()
    multiply(5)
    multiply(4)
    reduces[0].step(3)
    reduces[5].start()
    x_s[3].finish()
    multiply(2)
    reduces[4].start()
    reduces[1].step(3)
    multiply(3)
    reduces[2].start()
    reduces[0].finish()
    reduces[3].start()
    reduces[4].step(1)
    reduces[1].finish()
    reduces[5].step(1)
    reduces[2].step(1)
    reduces[3].step(1)
    reduces[4].step(2)
    reduces[5].step(2)
    reduces[2].step(2)
    reduces[3].step(2)
    reduces[4].step(3)
    reduces[5].step(3)
    reduces[2].step(3)
    reduces[3].step(3)
    reduces[4].finish()
    reduces[5].finish()
    reduces[2].finish()
    reduces[3].finish()

    last_row = pl.ds(SK, 1)
    store(off2.at[:, last_row], off2_out.at[:, last_row])
    store(diag1, diag1_out)
    store(diag2, diag2_out)
    for sent, sem in drains:
        take(sent, sem)
    for c in stores:
        c.wait()


def hand_over(*refs):
    n = len(refs) // 2
    for a, b in zip(refs[:n], refs[n:]):
        b[...] = a[...]


def on_device(anc_inverse, struct_one, lower_one, pivot_inv_one, lower_two, pivot_inv_two):
    tile = (TR, TC)

    def vmem(*lead):
        return pltpu.VMEM(lead + tile, F32)

    whole = pl.BlockSpec(memory_space=pltpu.VMEM)
    there = pl.BlockSpec(memory_space=pl.ANY)
    outs = tuple(
        jax.ShapeDtypeStruct(lead + tile, F32)
        for lead in ((NM, SK), (NM,), (NJ, SK + 1), (NJ,))
    )
    made = pl.pallas_call(
        kernel,
        out_shape=outs,
        in_specs=[pl.BlockSpec(memory_space=pltpu.SMEM)] + [there] * 5,
        out_specs=(there,) * 4,
        scratch_shapes=[
            vmem(NM, SK),
            vmem(NM),
            vmem(NJ, SK + 1),
            vmem(NJ),
            vmem(NA_LEAF, NA_ALL),
            vmem(NJ, SK),
            vmem(NJ),
            pltpu.VMEM((NY, 8, TC), I32),
            vmem(NX, NL + NM),
            vmem(NX, NJ),
            vmem(NX, NM, NC * SK),
            vmem(NX, NM, BLK),
            vmem(NR, NJ),
            vmem(NR, NL),
            vmem(NR, NJ, SK),
            vmem(NY, NM, BLK),
            vmem(NM, BLK),
            vmem(NM, 2, BLK),
            pltpu.VMEM((SK * TR, 2 * TC), F32),
            pltpu.VMEM((SK * TR, TC), F32),
            vmem(NJ),
            vmem(2, NJ, NZ, GT),
            vmem(NJ, NZ, GT),
            vmem(NJ, 4, GT),
            vmem(NJ, 4, GT),
            vmem(NJ, 4, GT),
            vmem(NJ, 4, GT),
            pltpu.SMEM((NY, 8, TC), I32),
            pltpu.SemaphoreType.DMA((N_OUT,)),
            pltpu.SemaphoreType.DMA((N_IN,)),
            pltpu.SemaphoreType.DMA((N_LOADS,)),
            pltpu.SemaphoreType.DMA,
            pltpu.SemaphoreType.DMA((N_STORES,)),
        ],
        compiler_params=pltpu.CompilerParams(
            collective_id=0, has_side_effects=True, vmem_limit_bytes=56 * 2**20
        ),
    )(
        struct_one,
        anc_inverse,
        lower_one.reshape(NL, TR, TC),
        pivot_inv_one,
        lower_two,
        pivot_inv_two,
    )
    return pl.pallas_call(
        hand_over,
        out_shape=outs,
        in_specs=[whole] * 4,
        out_specs=(whole,) * 4,
    )(*made)


def solution(mesh):
    placed = (
        P("leaf", None, "row", "col"),
        P("leaf", None),
        P("leaf", None, "row", "col"),
        P("leaf", "row", "col"),
        P("leaf", None, "row", "col"),
        P("leaf", "row", "col"),
    )
    return jax.shard_map(
        on_device,
        mesh=mesh,
        in_specs=placed,
        out_specs=(
            P("leaf", None, "row", "col"),
            P("leaf", "row", "col"),
            P("leaf", None, "row", "col"),
            P("leaf", "row", "col"),
        ),
        check_vma=False,
    )
```

```python
import jax
import jax.numpy as jnp
from jax import lax
from jax.experimental import pallas as pl
from jax.experimental.pallas import tpu as pltpu
from jax.sharding import PartitionSpec as P

F32 = jnp.float32
BF16 = jnp.bfloat16
I32 = jnp.int32
MESH = pl.DeviceIdType.MESH
TR = 32
TC = 128
NM = 3
SK = 5
NC = 2
NJ = NM * NC
NL = NM * SK
NX = 4
NY = 4
NZ = 8
NR = 2 * NZ
NA_LEAF = 6
NA_ALL = 24
BLK = SK * SK
UNITS = ((0, 13), (13, 12))
HALF = (7, 6)
GT = 3
N_OUT = 42
N_IN = 220
N_LOADS = 8
N_STORES = NM + NJ + 3


def split(a):
    hi = a.astype(BF16)
    return hi, (a - hi.astype(F32)).astype(BF16)


def dot3(a, b, lhs_dim):
    ah, al = split(a)
    bh, bl = split(b)

    def one(u, v):
        return lax.dot_general(
            u, v, (((lhs_dim,), (0,)), ((), ())), preferred_element_type=F32
        )

    return one(ah, bh) + (one(ah, bl) + one(al, bh))


def kernel(
    st, g_in, low1, piv1, low2, piv2,
    off1_out, diag1_out, off2_out, diag2_out,
    off1, diag1, off2, diag2,
    gv, av, p2, sv, xl, xb, xa, x3, zb, zl, za, ysel, yo, yn,
    zacc0, zacc1, pb, gp, sr, send_r, send_l, in_r, in_l,
    sm, ssem, rsem, lsem, msem, osem,
):
    y = lax.axis_index("leaf")
    r = lax.axis_index("row")
    x = lax.axis_index("col")
    z = r // 2
    h = r % 2

    def wrap(v, n):
        return lax.rem(v + n, n)

    def zrow(zz):
        return 2 * wrap(zz, NZ) + h

    x_right, x_left = (y, r, wrap(x + 1, NX)), (y, r, wrap(x - 1, NX))
    y_right, y_left = (wrap(y + 1, NY), r, x), (wrap(y - 1, NY), r, x)
    y_far = (wrap(y + 2, NY), r, x)
    z_right, z_left = (y, zrow(z + 1), x), (y, zrow(z - 1), x)
    sibling = (y, 2 * z + 1 - h, x)

    outs, ins, drains = [], [], []

    def next_out(sent):
        sem = ssem.at[len(outs)]
        outs.append(sem)
        drains.append((sent, sem))
        return sem

    def next_in():
        sem = rsem.at[len(ins)]
        ins.append(sem)
        return sem

    def take(ref, sem):
        pltpu.make_async_copy(ref, ref, sem).wait()

    def send(src, dst, to, out, into):
        c = pltpu.make_async_remote_copy(
            src_ref=src, dst_ref=dst, send_sem=out, recv_sem=into,
            device_id=to, device_id_type=MESH,
        )
        c.start()
        return c

    loads = [
        (low2.at[:, SK], zb.at[r]),
        (low1, xl.at[x, pl.ds(0, NL)]),
        (piv1, xl.at[x, pl.ds(NL, NM)]),
        (low1, zl.at[r]),
        (low2.at[:, SK], xb.at[x]),
        (g_in, gv),
        (low2.at[:, pl.ds(0, SK)], av),
        (piv2, p2),
    ]
    loads = [pltpu.make_async_copy(a, b, lsem.at[i]) for i, (a, b) in enumerate(loads)]
    for c in loads:
        c.start()
    lane = lax.broadcasted_iota(I32, (8, TC), 1)
    listed = jnp.zeros((8, TC), I32)
    for m in range(NM):
        for p in range(SK):
            listed = jnp.where(lane == m * SK + p, st[m, p], listed)
    sv[y] = listed

    barrier = pltpu.get_barrier_semaphore()
    partners = (x_right, x_left, y_right, y_left, y_far, z_right, z_left, sibling)
    for d in partners:
        pl.semaphore_signal(barrier, inc=1, device_id=d, device_id_type=MESH)
    pl.semaphore_wait(barrier, len(partners))

    class XRing:
        def __init__(self, at, n, half):
            self.at, self.n, self.half = at, n, half

        def start(self):
            self.out = next_out(self.at(pl.ds(0, 3)))
            own = self.at(x)
            self.a = send(own, own, x_right, self.out, next_in())
            self.b = send(own, own, x_left, self.out, next_in())

        def second(self):
            self.a.wait_recv()
            a = self.at(wrap(x - 1, NX)).at[pl.ds(0, self.half)]
            self.a = send(a, a, x_right, self.out, next_in())
            self.b.wait_recv()
            b = self.at(wrap(x + 1, NX)).at[pl.ds(self.half, self.n - self.half)]
            self.b = send(b, b, x_left, self.out, next_in())

        def finish(self):
            self.a.wait_recv()
            self.b.wait_recv()

    class ZRing:
        def __init__(self, at, n, half):
            self.at, self.n, self.half = at, n, half

        def start(self):
            self.out = next_out(self.at(pl.ds(0, 2 * NZ - 1)))
            self.sib = next_in()
            own = self.at(r)
            self.a = send(own, own, z_right, self.out, next_in())
            self.b = send(own, own, z_left, self.out, next_in())
            send(own, own, sibling, self.out, self.sib)

        def step(self, i):
            self.a.wait_recv()
            a = self.at(zrow(z - i))
            part = a.at[pl.ds(0, self.half)] if i == 3 else a
            self.a = send(part, part, z_right, self.out, next_in())
            self.b.wait_recv()
            b = self.at(zrow(z + i))
            part = b.at[pl.ds(self.half, self.n - self.half)] if i == 3 else b
            self.b = send(part, part, z_left, self.out, next_in())
            send(a, a, sibling, self.out, self.sib)
            send(b, b, sibling, self.out, self.sib)

        def last(self):
            self.a.wait_recv()
            self.b.wait_recv()
            far = self.at(zrow(z + 4))
            send(far, far, sibling, self.out, self.sib)

        def finish(self):
            take(self.at(pl.ds(0, NZ)), self.sib)

    z_b = [
        ZRing(lambda i, m=m: zb.at[i, pl.ds(m * NC, NC)], NC, 1) for m in range(NM)
    ]
    z_l = [
        ZRing(lambda i, m=m: zl.at[i, pl.ds(m * SK, SK)], SK, 2 + m % 2)
        for m in range(NM)
    ]
    z_a = [ZRing(lambda i, j=j: za.at[i, j], SK, 2 + j % 2) for j in range(NJ)]
    x_lp = XRing(lambda i: xl.at[i], NL + NM, (NL + NM) // 2)
    x_b = XRing(lambda i: xb.at[i], NJ, NJ // 2)
    x_a = [XRing(lambda i, m=m: xa.at[i, m], NC * SK, SK) for m in range(NM)]
    x_s = [
        XRing(lambda i, k=k: x3.at[i, k // 2, pl.ds(*UNITS[k % 2])], UNITS[k % 2][1], HALF[k % 2])
        for k in range(2 * NM)
    ]

    listed_in = next_in()

    def send_lists():
        out = next_out(sv.at[pl.ds(0, NY - 1)])
        own = sv.at[y]
        for d in (y_right, y_left, y_far):
            send(own, own, d, out, listed_in)

    def take_lists():
        take(sv.at[pl.ds(0, NY - 1)], listed_in)
        to_scalars = pltpu.make_async_copy(sv, sm, msem)
        to_scalars.start()
        to_scalars.wait()

    def select(delta, k):
        m, (first, count) = k // 2, UNITS[k % 2]
        to = wrap(y + delta, NY)

        def tile_of(e, carry):
            sq = sm[to, 0, m * SK + e // SK]
            sp = sm[to, 0, m * SK + lax.rem(e, SK)]
            mine = sp // NA_LEAF == y
            a = jnp.clip(sp - y * NA_LEAF, 0, NA_LEAF - 1)
            tile = gv[a, sq]
            ysel[delta, m, e] = jnp.where(mine, tile, jnp.zeros_like(tile))
            return carry

        lax.fori_loop(first, first + count, tile_of, 0)

    def halves(k):
        first, count = UNITS[k % 2]
        half = HALF[k % 2]
        return pl.ds(first, half), pl.ds(first + half, count - half)

    y_out = [next_out(ysel.at[pl.ds(0, 3), 0, pl.ds(0, n)]) for _, n in UNITS * NM]
    far_in = [next_in() for _ in range(2 * NM)]
    near_in = [next_in() for _ in range(2 * NM)]

    def y_far_half(k):
        select(2, k)
        m, (lo, hi) = k // 2, halves(k)
        send(ysel.at[2, m, lo], yo.at[m, lo], y_right, y_out[k], far_in[k])
        send(ysel.at[2, m, hi], yo.at[m, hi], y_left, y_out[k], far_in[k])

    def y_near_half(k):
        m, (lo, hi) = k // 2, halves(k)
        select(1, k)
        send(ysel.at[1, m, hi], yn.at[m, 0, hi], y_right, y_out[k], near_in[k])
        select(3, k)
        send(ysel.at[3, m, lo], yn.at[m, 1, lo], y_left, y_out[k], near_in[k])

    def y_merge(k):
        m, (lo, hi) = k // 2, halves(k)
        take(yo.at[m, pl.ds(*UNITS[k % 2])], far_in[k])
        ysel[1, m, lo] = ysel[1, m, lo] + yo[m, lo]
        send(ysel.at[1, m, lo], yn.at[m, 0, lo], y_right, y_out[k], near_in[k])
        ysel[3, m, hi] = ysel[3, m, hi] + yo[m, hi]
        send(ysel.at[3, m, hi], yn.at[m, 1, hi], y_left, y_out[k], near_in[k])

    def y_last(k):
        m, tiles = k // 2, pl.ds(*UNITS[k % 2])
        take(yn.at[m, :, tiles], near_in[k])
        x3[x, m, tiles] = ysel[0, m, tiles] + yn[m, 0, tiles] + yn[m, 1, tiles]
        x_s[k].start()

    def wide(tiles):
        return jnp.concatenate([t.reshape(-1, TC) for t in tiles], axis=1)

    def tall(tiles):
        return tiles.reshape(NR * TR, TC)

    stores = []

    def store(src, dst):
        c = pltpu.make_async_copy(src, dst, osem.at[len(stores)])
        c.start()
        stores.append(c)

    def low_cols(m):
        return wide([xl[i, m * SK : (m + 1) * SK] for i in range(NX)])

    def correct(m):
        lhs = jnp.concatenate(
            [low_cols(m), wide([xl[i, NL + m] for i in range(NX)])], axis=0
        )
        rhs = jnp.concatenate([tall(zb[:, m * NC + c]) for c in range(NC)], axis=1)
        prod = dot3(lhs, rhs, 1)
        for c in range(NC):
            j = m * NC + c
            part = prod[:, c * TC : (c + 1) * TC]
            fixed = av[j] - part[: SK * TR].reshape(SK, TR, TC)
            xa[x, m, c * SK : (c + 1) * SK] = fixed
            za[r, j] = fixed
            pb[j] = part[SK * TR :]

    def multiply(j):
        m, c = j // NC, j % NC
        zacc = zacc1 if c else zacc0
        zacc[...] = jnp.zeros_like(zacc)

        def block(q, carry):
            lhs = wide([x3[i, m, pl.ds(q * SK, SK)] for i in range(NX)])
            rhs = tall(za[:, j, q])
            if c == 0:
                rhs = jnp.concatenate([tall(zl[:, m * SK + q]), rhs], axis=1)
            zacc[...] += dot3(lhs, rhs, 1)
            return carry

        lax.fori_loop(0, SK, block, 0)
        own = zacc[:, (1 - c) * TC : (2 - c) * TC] if c == 0 else zacc[...]
        left = dot3(low_cols(m), zacc[...], 0)
        parts = [left[:, b * TC : (b + 1) * TC] for b in range(2 - c)]
        lhs = jnp.concatenate(
            [
                wide([xa[i, m, c * SK : (c + 1) * SK] for i in range(NX)]),
                wide([xb[i, j] for i in range(NX)]),
            ],
            axis=0,
        )
        parts.append(dot3(lhs, jnp.concatenate([own, pb[j]], axis=0), 0))
        for b, part in enumerate(parts):
            tiles = part.reshape(NZ, 2, TR, TC)
            for hh in range(2):
                gp[hh, j, :, b] = tiles[:, hh]
        reduces[j].share()
        off2[j, 0:SK] = -own.reshape(SK, TR, TC)
        upper = pl.ds(0, SK)
        store(off2.at[j, upper], off2_out.at[j, upper])
        if c == 0:
            off1[m] = -zacc[:, 0:TC].reshape(SK, TR, TC)
            store(off1.at[m], off1_out.at[m])

    class Reduce:
        def __init__(self, j):
            self.j, self.m, self.c = j, j // NC, j % NC
            self.n = 3 - self.c
            self.half = 1 if self.c or self.m % 2 else 2

        def mine(self, zz, a=0, b=None):
            zz = wrap(zz, NZ)
            b = self.n if b is None else b
            return gp[h, self.j, zz, a:b] + sr[self.j, zz, a:b]

        def share(self):
            part = pl.ds(0, self.n)
            out = next_out(gp.at[0, self.j, :, part])
            self.s = send(
                gp.at[1 - h, self.j, :, part],
                sr.at[self.j, :, part],
                sibling,
                out,
                next_in(),
            )

        def start(self):
            j, n, k = self.j, self.n, self.half
            self.out = next_out(gp.at[0, j, pl.ds(0, NZ - 1), pl.ds(0, n)])
            self.s.wait_recv()
            a, b = pl.ds(0, k), pl.ds(k, n - k)
            send_r[j, 0, 0:k] = self.mine(z + 4, 0, k)
            self.a = send(
                send_r.at[j, 0, a], in_r.at[j, 0, a], z_right, self.out, next_in()
            )
            send_l[j, 0, k:n] = self.mine(z - 4, k, n)
            self.b = send(
                send_l.at[j, 0, b], in_l.at[j, 0, b], z_left, self.out, next_in()
            )

        def step(self, s):
            j, n, k = self.j, self.n, self.half
            every = pl.ds(0, n)
            self.a.wait_recv()
            if s == 1:
                send_r[j, 1, 0:k] = in_r[j, 0, 0:k] + self.mine(z + 3, 0, k)
                send_r[j, 1, k:n] = self.mine(z + 3, k, n)
            else:
                send_r[j, s, 0:n] = in_r[j, s - 1, 0:n] + self.mine(z + 4 - s)
            self.a = send(
                send_r.at[j, s, every], in_r.at[j, s, every], z_right, self.out, next_in()
            )
            self.b.wait_recv()
            if s == 1:
                send_l[j, 1, 0:k] = self.mine(z - 3, 0, k)
                send_l[j, 1, k:n] = in_l[j, 0, k:n] + self.mine(z - 3, k, n)
            else:
                send_l[j, s, 0:n] = in_l[j, s - 1, 0:n] + self.mine(z - 4 + s)
            self.b = send(
                send_l.at[j, s, every], in_l.at[j, s, every], z_left, self.out, next_in()
            )

        def finish(self):
            j, m, c, n = self.j, self.m, self.c, self.n
            self.a.wait_recv()
            self.b.wait_recv()
            total = in_r[j, 3, 0:n] + in_l[j, 3, 0:n] + self.mine(z)
            if c == 0:
                diag1[m] = xl[x, NL + m] + total[0]
            off2[j, SK] = total[n - 2] - pb[j]
            diag2[j] = p2[j] + total[n - 1]

    reduces = [Reduce(j) for j in range(NJ)]

    for c in loads:
        c.wait()

    send_lists()
    z_b[0].start()
    z_b[1].start()
    x_lp.start()
    z_b[2].start()
    z_l[0].start()
    z_l[1].start()
    z_l[2].start()
    take_lists()
    select(0, 4)
    y_far_half(0)
    select(0, 1)
    z_b[0].step(1)
    y_near_half(0)
    select(0, 2)
    z_b[2].step(1)
    select(0, 0)
    select(0, 5)
    select(0, 3)
    z_b[1].step(1)
    z_l[1].step(1)
    x_b.start()
    y_merge(0)
    y_far_half(1)
    z_b[0].step(2)
    x_lp.second()
    z_l[2].step(1)
    y_near_half(1)
    z_b[1].step(2)
    z_b[2].step(2)
    x_b.second()
    z_b[0].step(3)
    y_last(0)
    z_l[2].step(2)
    x_lp.finish()
    z_b[2].step(3)
    z_b[0].last()
    z_l[0].step(1)
    z_b[1].step(3)
    z_b[0].finish()
    correct(0)
    x_a[0].start()
    z_a[1].start()
    z_a[0].start()
    z_l[2].step(3)
    z_b[2].last()
    y_merge(1)
    y_far_half(2)
    y_near_half(2)
    x_s[0].second()
    z_b[1].last()
    z_l[0].step(2)
    z_b[2].finish()
    correct(2)
    z_a[4].start()
    z_a[1].step(1)
    x_a[2].start()
    x_b.finish()
    y_last(1)
    z_a[0].step(1)
    x_a[0].second()
    x_s[0].finish()
    y_merge(2)
    y_far_half(3)
    y_near_half(3)
    z_l[0].step(3)
    z_a[4].step(1)
    x_a[2].second()
    z_a[1].step(2)
    z_a[0].step(2)
    y_last(2)
    x_s[1].second()
    y_merge(3)
    z_l[0].last()
    z_a[4].step(2)
    x_a[0].finish()
    z_l[0].finish()
    y_far_half(4)
    y_near_half(4)
    z_a[5].start()
    z_a[1].step(3)
    z_l[1].step(2)
    z_a[0].step(3)
    y_last(3)
    z_a[4].step(3)
    z_l[2].last()
    x_a[2].finish()
    z_b[1].finish()
    correct(1)
    z_a[3].start()
    z_a[2].start()
    y_merge(4)
    y_far_half(5)
    x_s[2].second()
    y_near_half(5)
    z_l[2].finish()
    z_a[5].step(1)
    x_s[1].finish()
    z_l[1].step(3)
    z_a[1].last()
    x_a[1].start()
    z_a[1].finish()
    z_a[4].last()
    z_a[0].last()
    y_last(4)
    z_a[0].finish()
    x_s[3].second()
    z_a[3].step(1)
    multiply(0)
    y_merge(5)
    x_s[2].finish()
    z_a[2].step(1)
    reduces[0].start()
    multiply(1)
    z_l[1].last()
    z_a[5].step(2)
    z_a[4].finish()
    z_l[1].finish()
    reduces[1].start()
    z_a[3].step(2)
    y_last(5)
    reduces[0].step(1)
    z_a[2].step(2)
    x_a[1].second()
    z_a[5].step(3)
    x_s[4].second()
    reduces[1].step(1)
    x_s[3].finish()
    z_a[3].step(3)
    reduces[0].step(2)
    z_a[2].step(3)
    z_a[5].last()
    reduces[1].step(2)
    x_s[5].second()
    z_a[3].last()
    z_a[5].finish()
    z_a[3].finish()
    reduces[0].step(3)
    z_a[2].last()
    x_a[1].finish()
    multiply(3)
    z_a[2].finish()
    x_s[4].finish()
    multiply(2)
    reduces[3].start()
    reduces[1].step(3)
    x_s[5].finish()
    multiply(4)
    reduces[2].start()
    reduces[0].finish()
    multiply(5)
    reduces[4].start()
    reduces[1].finish()
    reduces[5].start()
    reduces[3].step(1)
    reduces[2].step(1)
    reduces[4].step(1)
    reduces[5].step(1)
    reduces[3].step(2)
    reduces[2].step(2)
    reduces[4].step(2)
    reduces[5].step(2)
    reduces[3].step(3)
    reduces[2].step(3)
    reduces[4].step(3)
    reduces[5].step(3)
    reduces[3].finish()
    reduces[2].finish()
    reduces[4].finish()
    reduces[5].finish()

    last_row = pl.ds(SK, 1)
    store(off2.at[:, last_row], off2_out.at[:, last_row])
    store(diag1, diag1_out)
    store(diag2, diag2_out)
    for sent, sem in drains:
        take(sent, sem)
    for c in stores:
        c.wait()


def hand_over(*refs):
    n = len(refs) // 2
    for a, b in zip(refs[:n], refs[n:]):
        b[...] = a[...]


def on_device(anc_inverse, struct_one, lower_one, pivot_inv_one, lower_two, pivot_inv_two):
    tile = (TR, TC)

    def vmem(*lead):
        return pltpu.VMEM(lead + tile, F32)

    whole = pl.BlockSpec(memory_space=pltpu.VMEM)
    there = pl.BlockSpec(memory_space=pl.ANY)
    outs = tuple(
        jax.ShapeDtypeStruct(lead + tile, F32)
        for lead in ((NM, SK), (NM,), (NJ, SK + 1), (NJ,))
    )
    made = pl.pallas_call(
        kernel,
        out_shape=outs,
        in_specs=[pl.BlockSpec(memory_space=pltpu.SMEM)] + [there] * 5,
        out_specs=(there,) * 4,
        scratch_shapes=[
            vmem(NM, SK),
            vmem(NM),
            vmem(NJ, SK + 1),
            vmem(NJ),
            vmem(NA_LEAF, NA_ALL),
            vmem(NJ, SK),
            vmem(NJ),
            pltpu.VMEM((NY, 8, TC), I32),
            vmem(NX, NL + NM),
            vmem(NX, NJ),
            vmem(NX, NM, NC * SK),
            vmem(NX, NM, BLK),
            vmem(NR, NJ),
            vmem(NR, NL),
            vmem(NR, NJ, SK),
            vmem(NY, NM, BLK),
            vmem(NM, BLK),
            vmem(NM, 2, BLK),
            pltpu.VMEM((SK * TR, 2 * TC), F32),
            pltpu.VMEM((SK * TR, TC), F32),
            vmem(NJ),
            vmem(2, NJ, NZ, GT),
            vmem(NJ, NZ, GT),
            vmem(NJ, 4, GT),
            vmem(NJ, 4, GT),
            vmem(NJ, 4, GT),
            vmem(NJ, 4, GT),
            pltpu.SMEM((NY, 8, TC), I32),
            pltpu.SemaphoreType.DMA((N_OUT,)),
            pltpu.SemaphoreType.DMA((N_IN,)),
            pltpu.SemaphoreType.DMA((N_LOADS,)),
            pltpu.SemaphoreType.DMA,
            pltpu.SemaphoreType.DMA((N_STORES,)),
        ],
        compiler_params=pltpu.CompilerParams(
            collective_id=0, has_side_effects=True, vmem_limit_bytes=56 * 2**20
        ),
    )(
        struct_one,
        anc_inverse,
        lower_one.reshape(NL, TR, TC),
        pivot_inv_one,
        lower_two,
        pivot_inv_two,
    )
    return pl.pallas_call(
        hand_over,
        out_shape=outs,
        in_specs=[whole] * 4,
        out_specs=(whole,) * 4,
    )(*made)


def solution(mesh):
    placed = (
        P("leaf", None, "row", "col"),
        P("leaf", None),
        P("leaf", None, "row", "col"),
        P("leaf", "row", "col"),
        P("leaf", None, "row", "col"),
        P("leaf", "row", "col"),
    )
    return jax.shard_map(
        on_device,
        mesh=mesh,
        in_specs=placed,
        out_specs=(
            P("leaf", None, "row", "col"),
            P("leaf", "row", "col"),
            P("leaf", None, "row", "col"),
            P("leaf", "row", "col"),
        ),
        check_vma=False,
    )
```

```python
import jax
import jax.numpy as jnp
from jax import lax
from jax.experimental import pallas as pl
from jax.experimental.pallas import tpu as pltpu
from jax.sharding import PartitionSpec as P

F32 = jnp.float32
BF16 = jnp.bfloat16
I32 = jnp.int32
MESH = pl.DeviceIdType.MESH
TR = 32
TC = 128
NM = 3
SK = 5
NC = 2
NJ = NM * NC
NL = NM * SK
NX = 4
NY = 4
NZ = 8
NR = 2 * NZ
NA_LEAF = 6
NA_ALL = 24
BLK = SK * SK
UNITS = ((0, 13), (13, 12))
HALF = (7, 6)
GT = 3
N_OUT = 42
N_IN = 220
N_LOADS = 8
N_STORES = NM + NJ + 3


def split(a):
    hi = a.astype(BF16)
    return hi, (a - hi.astype(F32)).astype(BF16)


def dot3(a, b, lhs_dim):
    ah, al = split(a)
    bh, bl = split(b)

    def one(u, v):
        return lax.dot_general(
            u, v, (((lhs_dim,), (0,)), ((), ())), preferred_element_type=F32
        )

    return one(ah, bh) + (one(ah, bl) + one(al, bh))


def kernel(
    st, g_in, low1, piv1, low2, piv2,
    off1_out, diag1_out, off2_out, diag2_out,
    off1, diag1, off2, diag2,
    gv, av, p2, sv, xl, xb, xa, x3, zb, zl, za, ysel, yo, yn,
    zacc, pb, gp, sr, send_r, send_l, in_r, in_l,
    sm, ssem, rsem, lsem, msem, osem,
):
    y = lax.axis_index("leaf")
    r = lax.axis_index("row")
    x = lax.axis_index("col")
    z = r // 2
    h = r % 2

    def wrap(v, n):
        return lax.rem(v + n, n)

    def zrow(zz):
        return 2 * wrap(zz, NZ) + h

    x_right, x_left = (y, r, wrap(x + 1, NX)), (y, r, wrap(x - 1, NX))
    y_right, y_left = (wrap(y + 1, NY), r, x), (wrap(y - 1, NY), r, x)
    y_far = (wrap(y + 2, NY), r, x)
    z_right, z_left = (y, zrow(z + 1), x), (y, zrow(z - 1), x)
    sibling = (y, 2 * z + 1 - h, x)

    outs, ins, drains = [], [], []

    def next_out(sent):
        sem = ssem.at[len(outs)]
        outs.append(sem)
        drains.append((sent, sem))
        return sem

    def next_in():
        sem = rsem.at[len(ins)]
        ins.append(sem)
        return sem

    def take(ref, sem):
        pltpu.make_async_copy(ref, ref, sem).wait()

    def send(src, dst, to, out, into):
        c = pltpu.make_async_remote_copy(
            src_ref=src, dst_ref=dst, send_sem=out, recv_sem=into,
            device_id=to, device_id_type=MESH,
        )
        c.start()
        return c

    loads = [
        (low2.at[:, SK], zb.at[r]),
        (low1, xl.at[x, pl.ds(0, NL)]),
        (piv1, xl.at[x, pl.ds(NL, NM)]),
        (low1, zl.at[r]),
        (low2.at[:, SK], xb.at[x]),
        (g_in, gv),
        (low2.at[:, pl.ds(0, SK)], av),
        (piv2, p2),
    ]
    loads = [pltpu.make_async_copy(a, b, lsem.at[i]) for i, (a, b) in enumerate(loads)]
    for c in loads:
        c.start()
    lane = lax.broadcasted_iota(I32, (8, TC), 1)
    listed = jnp.zeros((8, TC), I32)
    for m in range(NM):
        for p in range(SK):
            listed = jnp.where(lane == m * SK + p, st[m, p], listed)
    sv[y] = listed

    barrier = pltpu.get_barrier_semaphore()
    partners = (x_right, x_left, y_right, y_left, y_far, z_right, z_left, sibling)
    for d in partners:
        pl.semaphore_signal(barrier, inc=1, device_id=d, device_id_type=MESH)
    pl.semaphore_wait(barrier, len(partners))

    class XRing:
        def __init__(self, at, n, half):
            self.at, self.n, self.half = at, n, half

        def start(self):
            self.out = next_out(self.at(pl.ds(0, 3)))
            own = self.at(x)
            self.a = send(own, own, x_right, self.out, next_in())
            self.b = send(own, own, x_left, self.out, next_in())

        def second(self):
            self.a.wait_recv()
            a = self.at(wrap(x - 1, NX)).at[pl.ds(0, self.half)]
            self.a = send(a, a, x_right, self.out, next_in())
            self.b.wait_recv()
            b = self.at(wrap(x + 1, NX)).at[pl.ds(self.half, self.n - self.half)]
            self.b = send(b, b, x_left, self.out, next_in())

        def finish(self):
            self.a.wait_recv()
            self.b.wait_recv()

    class ZRing:
        def __init__(self, at, n, half):
            self.at, self.n, self.half = at, n, half

        def start(self):
            self.out = next_out(self.at(pl.ds(0, 2 * NZ - 1)))
            self.sib = next_in()
            own = self.at(r)
            self.a = send(own, own, z_right, self.out, next_in())
            self.b = send(own, own, z_left, self.out, next_in())
            send(own, own, sibling, self.out, self.sib)

        def step(self, i):
            self.a.wait_recv()
            a = self.at(zrow(z - i))
            part = a.at[pl.ds(0, self.half)] if i == 3 else a
            self.a = send(part, part, z_right, self.out, next_in())
            self.b.wait_recv()
            b = self.at(zrow(z + i))
            part = b.at[pl.ds(self.half, self.n - self.half)] if i == 3 else b
            self.b = send(part, part, z_left, self.out, next_in())
            send(a, a, sibling, self.out, self.sib)
            send(b, b, sibling, self.out, self.sib)

        def last(self):
            self.a.wait_recv()
            self.b.wait_recv()
            far = self.at(zrow(z + 4))
            send(far, far, sibling, self.out, self.sib)

        def finish(self):
            take(self.at(pl.ds(0, NZ)), self.sib)

    z_b = [
        ZRing(lambda i, m=m: zb.at[i, pl.ds(m * NC, NC)], NC, 1) for m in range(NM)
    ]
    z_l = [
        ZRing(lambda i, m=m: zl.at[i, pl.ds(m * SK, SK)], SK, 2 + m % 2)
        for m in range(NM)
    ]
    z_a = [ZRing(lambda i, j=j: za.at[i, j], SK, 2 + j % 2) for j in range(NJ)]
    x_lp = XRing(lambda i: xl.at[i], NL + NM, (NL + NM) // 2)
    x_b = XRing(lambda i: xb.at[i], NJ, NJ // 2)
    x_a = [XRing(lambda i, m=m: xa.at[i, m], NC * SK, SK) for m in range(NM)]
    x_s = [
        XRing(lambda i, k=k: x3.at[i, k // 2, pl.ds(*UNITS[k % 2])], UNITS[k % 2][1], HALF[k % 2])
        for k in range(2 * NM)
    ]

    listed_in = next_in()

    def send_lists():
        out = next_out(sv.at[pl.ds(0, NY - 1)])
        own = sv.at[y]
        for d in (y_right, y_left, y_far):
            send(own, own, d, out, listed_in)

    def take_lists():
        take(sv.at[pl.ds(0, NY - 1)], listed_in)
        to_scalars = pltpu.make_async_copy(sv, sm, msem)
        to_scalars.start()
        to_scalars.wait()

    def select(delta, k):
        m, (first, count) = k // 2, UNITS[k % 2]
        to = wrap(y + delta, NY)

        def tile_of(e, carry):
            sq = sm[to, 0, m * SK + e // SK]
            sp = sm[to, 0, m * SK + lax.rem(e, SK)]
            mine = sp // NA_LEAF == y
            a = jnp.clip(sp - y * NA_LEAF, 0, NA_LEAF - 1)
            tile = gv[a, sq]
            ysel[delta, m, e] = jnp.where(mine, tile, jnp.zeros_like(tile))
            return carry

        lax.fori_loop(first, first + count, tile_of, 0)

    def halves(k):
        first, count = UNITS[k % 2]
        half = HALF[k % 2]
        return pl.ds(first, half), pl.ds(first + half, count - half)

    y_out = [next_out(ysel.at[pl.ds(0, 3), 0, pl.ds(0, n)]) for _, n in UNITS * NM]
    far_in = [next_in() for _ in range(2 * NM)]
    near_in = [next_in() for _ in range(2 * NM)]

    def y_far_half(k):
        select(2, k)
        m, (lo, hi) = k // 2, halves(k)
        send(ysel.at[2, m, lo], yo.at[m, lo], y_right, y_out[k], far_in[k])
        send(ysel.at[2, m, hi], yo.at[m, hi], y_left, y_out[k], far_in[k])

    def y_near_half(k):
        m, (lo, hi) = k // 2, halves(k)
        select(1, k)
        send(ysel.at[1, m, hi], yn.at[m, 0, hi], y_right, y_out[k], near_in[k])
        select(3, k)
        send(ysel.at[3, m, lo], yn.at[m, 1, lo], y_left, y_out[k], near_in[k])

    def y_merge(k):
        m, (lo, hi) = k // 2, halves(k)
        take(yo.at[m, pl.ds(*UNITS[k % 2])], far_in[k])
        ysel[1, m, lo] = ysel[1, m, lo] + yo[m, lo]
        send(ysel.at[1, m, lo], yn.at[m, 0, lo], y_right, y_out[k], near_in[k])
        ysel[3, m, hi] = ysel[3, m, hi] + yo[m, hi]
        send(ysel.at[3, m, hi], yn.at[m, 1, hi], y_left, y_out[k], near_in[k])

    def y_last(k):
        m, tiles = k // 2, pl.ds(*UNITS[k % 2])
        take(yn.at[m, :, tiles], near_in[k])
        x3[x, m, tiles] = ysel[0, m, tiles] + yn[m, 0, tiles] + yn[m, 1, tiles]
        x_s[k].start()

    def wide(tiles):
        return jnp.concatenate([t.reshape(-1, TC) for t in tiles], axis=1)

    def tall(tiles):
        return tiles.reshape(NR * TR, TC)

    stores = []

    def store(src, dst):
        c = pltpu.make_async_copy(src, dst, osem.at[len(stores)])
        c.start()
        stores.append(c)

    def low_cols(m):
        return wide([xl[i, m * SK : (m + 1) * SK] for i in range(NX)])

    def correct(m):
        lhs = jnp.concatenate(
            [low_cols(m), wide([xl[i, NL + m] for i in range(NX)])], axis=0
        )
        rhs = jnp.concatenate([tall(zb[:, m * NC + c]) for c in range(NC)], axis=1)
        prod = dot3(lhs, rhs, 1)
        for c in range(NC):
            j = m * NC + c
            part = prod[:, c * TC : (c + 1) * TC]
            fixed = av[j] - part[: SK * TR].reshape(SK, TR, TC)
            xa[x, m, c * SK : (c + 1) * SK] = fixed
            za[r, j] = fixed
            pb[j] = part[SK * TR :]

    def spread(j, parts):
        for b, part in enumerate(parts):
            tiles = part.reshape(NZ, 2, TR, TC)
            for hh in range(2):
                gp[hh, j, :, b] = tiles[:, hh]
        reduces[j].share()

    def multiply(m):
        acc = zacc.at[m]
        acc[...] = jnp.zeros(acc.shape, F32)

        def block(q, carry):
            lhs = wide([x3[i, m, pl.ds(q * SK, SK)] for i in range(NX)])
            rhs = jnp.concatenate(
                [tall(zl[:, m * SK + q])]
                + [tall(za[:, m * NC + c, q]) for c in range(NC)],
                axis=1,
            )
            acc[...] += dot3(lhs, rhs, 1)
            return carry

        lax.fori_loop(0, SK, block, 0)
        left = dot3(low_cols(m), acc[...], 0)
        spread(2 * m, [left[:, b * TC : (b + 1) * TC] for b in range(1 + NC)])
        off1[m] = -acc[:, 0:TC].reshape(SK, TR, TC)
        store(off1.at[m], off1_out.at[m])
        upper = pl.ds(0, SK)
        for c in range(NC):
            j = m * NC + c
            off2[j, 0:SK] = -acc[:, (c + 1) * TC : (c + 2) * TC].reshape(SK, TR, TC)
            store(off2.at[j, upper], off2_out.at[j, upper])

    def multiply_own(m):
        parts = []
        for c in range(NC):
            j = m * NC + c
            lhs = jnp.concatenate(
                [
                    wide([xa[i, m, c * SK : (c + 1) * SK] for i in range(NX)]),
                    wide([xb[i, j] for i in range(NX)]),
                ],
                axis=0,
            )
            rhs = jnp.concatenate(
                [zacc[m, :, (c + 1) * TC : (c + 2) * TC], pb[j]], axis=0
            )
            parts.append(dot3(lhs, rhs, 0))
        spread(2 * m + 1, parts)

    class Reduce:
        def __init__(self, j):
            self.j, self.m, self.c = j, j // 2, j % 2
            self.n = 3 - self.c
            self.half = 1 if self.c or self.m % 2 else 2

        def mine(self, zz, a=0, b=None):
            zz = wrap(zz, NZ)
            b = self.n if b is None else b
            return gp[h, self.j, zz, a:b] + sr[self.j, zz, a:b]

        def share(self):
            part = pl.ds(0, self.n)
            out = next_out(gp.at[0, self.j, :, part])
            self.s = send(
                gp.at[1 - h, self.j, :, part],
                sr.at[self.j, :, part],
                sibling,
                out,
                next_in(),
            )

        def start(self):
            j, n, k = self.j, self.n, self.half
            self.out = next_out(gp.at[0, j, pl.ds(0, NZ - 1), pl.ds(0, n)])
            self.s.wait_recv()
            a, b = pl.ds(0, k), pl.ds(k, n - k)
            send_r[j, 0, 0:k] = self.mine(z + 4, 0, k)
            self.a = send(
                send_r.at[j, 0, a], in_r.at[j, 0, a], z_right, self.out, next_in()
            )
            send_l[j, 0, k:n] = self.mine(z - 4, k, n)
            self.b = send(
                send_l.at[j, 0, b], in_l.at[j, 0, b], z_left, self.out, next_in()
            )

        def step(self, s):
            j, n, k = self.j, self.n, self.half
            every = pl.ds(0, n)
            self.a.wait_recv()
            if s == 1:
                send_r[j, 1, 0:k] = in_r[j, 0, 0:k] + self.mine(z + 3, 0, k)
                send_r[j, 1, k:n] = self.mine(z + 3, k, n)
            else:
                send_r[j, s, 0:n] = in_r[j, s - 1, 0:n] + self.mine(z + 4 - s)
            self.a = send(
                send_r.at[j, s, every], in_r.at[j, s, every], z_right, self.out, next_in()
            )
            self.b.wait_recv()
            if s == 1:
                send_l[j, 1, 0:k] = self.mine(z - 3, 0, k)
                send_l[j, 1, k:n] = in_l[j, 0, k:n] + self.mine(z - 3, k, n)
            else:
                send_l[j, s, 0:n] = in_l[j, s - 1, 0:n] + self.mine(z - 4 + s)
            self.b = send(
                send_l.at[j, s, every], in_l.at[j, s, every], z_left, self.out, next_in()
            )

        def finish(self):
            j, m, c, n = self.j, self.m, self.c, self.n
            self.a.wait_recv()
            self.b.wait_recv()
            total = in_r[j, 3, 0:n] + in_l[j, 3, 0:n] + self.mine(z)
            if c == 0:
                diag1[m] = xl[x, NL + m] + total[0]
                for i in range(NC):
                    off2[m * NC + i, SK] = total[1 + i] - pb[m * NC + i]
            else:
                for i in range(NC):
                    diag2[m * NC + i] = p2[m * NC + i] + total[i]

    reduces = [Reduce(j) for j in range(2 * NM)]

    for c in loads:
        c.wait()

    send_lists()
    z_b[0].start()
    z_l[0].start()
    z_b[1].start()
    x_lp.start()
    z_l[1].start()
    take_lists()
    y_far_half(0)
    z_b[0].step(1)
    z_b[2].start()
    z_b[1].step(1)
    z_l[0].step(1)
    select(0, 4)
    y_near_half(0)
    x_b.start()
    select(0, 5)
    z_b[2].step(1)
    z_b[0].step(2)
    y_merge(0)
    y_far_half(1)
    x_lp.second()
    z_l[2].start()
    z_b[1].step(2)
    y_near_half(1)
    x_b.second()
    z_b[2].step(2)
    z_b[0].step(3)
    select(0, 0)
    z_l[0].step(2)
    select(0, 1)
    y_last(0)
    z_l[2].step(1)
    select(0, 3)
    z_b[0].last()
    z_b[1].step(3)
    z_l[1].step(1)
    y_merge(1)
    y_far_half(2)
    z_b[0].finish()
    x_lp.finish()
    correct(0)
    z_a[1].start()
    z_a[0].start()
    x_a[0].start()
    z_b[1].last()
    y_near_half(2)
    z_l[0].step(3)
    z_b[2].step(3)
    y_last(1)
    z_l[1].step(2)
    z_b[1].finish()
    correct(1)
    z_a[2].start()
    y_merge(2)
    y_far_half(3)
    z_a[0].step(1)
    select(0, 2)
    x_a[1].start()
    z_b[2].last()
    x_s[0].second()
    z_a[1].step(1)
    z_l[0].last()
    z_a[3].start()
    z_b[2].finish()
    z_a[2].step(1)
    z_l[1].step(3)
    y_near_half(3)
    y_last(2)
    y_merge(3)
    z_a[1].step(2)
    y_far_half(4)
    x_a[1].second()
    z_a[0].step(2)
    z_a[2].step(2)
    correct(2)
    y_near_half(4)
    y_last(3)
    z_a[5].start()
    x_s[2].second()
    z_l[0].finish()
    z_a[4].start()
    x_s[1].second()
    z_a[3].step(1)
    y_merge(4)
    z_a[1].step(3)
    y_far_half(5)
    x_a[0].second()
    y_near_half(5)
    z_a[2].step(3)
    z_a[0].step(3)
    x_b.finish()
    z_a[5].step(1)
    y_last(4)
    z_l[1].last()
    z_a[1].last()
    z_a[3].step(2)
    x_s[2].finish()
    x_s[0].finish()
    z_a[4].step(1)
    y_merge(5)
    z_l[2].step(2)
    z_a[0].last()
    z_a[0].finish()
    z_a[2].last()
    x_s[1].finish()
    z_a[1].finish()
    x_s[3].second()
    z_a[5].step(2)
    x_a[0].finish()
    multiply(0)
    z_a[3].step(3)
    y_last(5)
    x_a[2].start()
    z_l[1].finish()
    reduces[0].start()
    multiply_own(0)
    z_a[4].step(2)
    z_l[2].step(3)
    reduces[1].start()
    x_s[4].second()
    reduces[0].step(1)
    z_a[5].step(3)
    z_a[3].last()
    z_a[3].finish()
    z_a[2].finish()
    x_s[5].second()
    reduces[1].step(1)
    z_a[4].step(3)
    x_s[3].finish()
    multiply(1)
    reduces[0].step(2)
    x_a[2].second()
    z_l[2].last()
    x_a[1].finish()
    multiply_own(1)
    reduces[1].step(2)
    z_a[4].last()
    reduces[2].start()
    reduces[3].start()
    z_l[2].finish()
    z_a[5].last()
    z_a[4].finish()
    reduces[0].step(3)
    z_a[5].finish()
    x_s[4].finish()
    x_s[5].finish()
    multiply(2)
    x_a[2].finish()
    reduces[3].step(1)
    multiply_own(2)
    reduces[4].start()
    reduces[5].start()
    reduces[2].step(1)
    reduces[3].step(2)
    reduces[4].step(1)
    reduces[5].step(1)
    reduces[2].step(2)
    reduces[1].step(3)
    reduces[4].step(2)
    reduces[5].step(2)
    reduces[0].finish()
    reduces[2].step(3)
    reduces[3].step(3)
    reduces[4].step(3)
    reduces[5].step(3)
    reduces[3].finish()
    reduces[1].finish()
    reduces[4].finish()
    reduces[2].finish()
    reduces[5].finish()

    last_row = pl.ds(SK, 1)
    store(off2.at[:, last_row], off2_out.at[:, last_row])
    store(diag1, diag1_out)
    store(diag2, diag2_out)
    for sent, sem in drains:
        take(sent, sem)
    for c in stores:
        c.wait()


def hand_over(*refs):
    n = len(refs) // 2
    for a, b in zip(refs[:n], refs[n:]):
        b[...] = a[...]


def on_device(anc_inverse, struct_one, lower_one, pivot_inv_one, lower_two, pivot_inv_two):
    tile = (TR, TC)

    def vmem(*lead):
        return pltpu.VMEM(lead + tile, F32)

    whole = pl.BlockSpec(memory_space=pltpu.VMEM)
    there = pl.BlockSpec(memory_space=pl.ANY)
    outs = tuple(
        jax.ShapeDtypeStruct(lead + tile, F32)
        for lead in ((NM, SK), (NM,), (NJ, SK + 1), (NJ,))
    )
    made = pl.pallas_call(
        kernel,
        out_shape=outs,
        in_specs=[pl.BlockSpec(memory_space=pltpu.SMEM)] + [there] * 5,
        out_specs=(there,) * 4,
        scratch_shapes=[
            vmem(NM, SK),
            vmem(NM),
            vmem(NJ, SK + 1),
            vmem(NJ),
            vmem(NA_LEAF, NA_ALL),
            vmem(NJ, SK),
            vmem(NJ),
            pltpu.VMEM((NY, 8, TC), I32),
            vmem(NX, NL + NM),
            vmem(NX, NJ),
            vmem(NX, NM, NC * SK),
            vmem(NX, NM, BLK),
            vmem(NR, NJ),
            vmem(NR, NL),
            vmem(NR, NJ, SK),
            vmem(NY, NM, BLK),
            vmem(NM, BLK),
            vmem(NM, 2, BLK),
            pltpu.VMEM((NM, SK * TR, (1 + NC) * TC), F32),
            vmem(NJ),
            vmem(2, NJ, NZ, GT),
            vmem(NJ, NZ, GT),
            vmem(NJ, 4, GT),
            vmem(NJ, 4, GT),
            vmem(NJ, 4, GT),
            vmem(NJ, 4, GT),
            pltpu.SMEM((NY, 8, TC), I32),
            pltpu.SemaphoreType.DMA((N_OUT,)),
            pltpu.SemaphoreType.DMA((N_IN,)),
            pltpu.SemaphoreType.DMA((N_LOADS,)),
            pltpu.SemaphoreType.DMA,
            pltpu.SemaphoreType.DMA((N_STORES,)),
        ],
        compiler_params=pltpu.CompilerParams(
            collective_id=0, has_side_effects=True, vmem_limit_bytes=56 * 2**20
        ),
    )(
        struct_one,
        anc_inverse,
        lower_one.reshape(NL, TR, TC),
        pivot_inv_one,
        lower_two,
        pivot_inv_two,
    )
    return pl.pallas_call(
        hand_over,
        out_shape=outs,
        in_specs=[whole] * 4,
        out_specs=(whole,) * 4,
    )(*made)


def solution(mesh):
    placed = (
        P("leaf", None, "row", "col"),
        P("leaf", None),
        P("leaf", None, "row", "col"),
        P("leaf", "row", "col"),
        P("leaf", None, "row", "col"),
        P("leaf", "row", "col"),
    )
    return jax.shard_map(
        on_device,
        mesh=mesh,
        in_specs=placed,
        out_specs=(
            P("leaf", None, "row", "col"),
            P("leaf", "row", "col"),
            P("leaf", None, "row", "col"),
            P("leaf", "row", "col"),
        ),
        check_vma=False,
    )
```

```python
import jax
import jax.numpy as jnp
from jax import lax
from jax.experimental import pallas as pl
from jax.experimental.pallas import tpu as pltpu
from jax.sharding import PartitionSpec as P

F32 = jnp.float32
BF16 = jnp.bfloat16
I32 = jnp.int32
MESH = pl.DeviceIdType.MESH
TR = 32
TC = 128
NM = 3
SK = 5
NC = 2
NJ = NM * NC
NL = NM * SK
NX = 4
NY = 4
NZ = 8
NR = 2 * NZ
NA_LEAF = 6
NA_ALL = 24
BLK = SK * SK
UNITS = ((0, 13), (13, 12))
HALF = (7, 6)
GT = 3
N_OUT = 42
N_IN = 130
N_LOADS = 8
N_STORES = NM + NJ + 3


def split(a):
    hi = a.astype(BF16)
    return hi, (a - hi.astype(F32)).astype(BF16)


def dot3(a, b, lhs_dim):
    ah, al = split(a)
    bh, bl = split(b)

    def one(u, v):
        return lax.dot_general(
            u, v, (((lhs_dim,), (0,)), ((), ())), preferred_element_type=F32
        )

    return one(ah, bh) + (one(ah, bl) + one(al, bh))


def kernel(
    st, g_in, low1, piv1, low2, piv2,
    off1_out, diag1_out, off2_out, diag2_out,
    off1, diag1, off2, diag2,
    gv, av, p2, sv, xl, xb, xa, x3, zb, zl, za, ysel, yo, yn,
    zacc, pb, gp, sr, send_r, send_l, in_r, in_l,
    sm, ssem, rsem, lsem, msem, osem,
):
    y = lax.axis_index("leaf")
    r = lax.axis_index("row")
    x = lax.axis_index("col")
    z = r // 2
    h = r % 2

    def wrap(v, n):
        return lax.rem(v + n, n)

    def zrow(zz):
        return 2 * wrap(zz, NZ) + h

    x_right, x_left = (y, r, wrap(x + 1, NX)), (y, r, wrap(x - 1, NX))
    y_right, y_left = (wrap(y + 1, NY), r, x), (wrap(y - 1, NY), r, x)
    y_far = (wrap(y + 2, NY), r, x)
    z_right, z_left = (y, zrow(z + 1), x), (y, zrow(z - 1), x)
    sibling = (y, 2 * z + 1 - h, x)

    outs, ins, drains = [], [], []

    def next_out(sent):
        sem = ssem.at[len(outs)]
        outs.append(sem)
        drains.append((sent, sem))
        return sem

    def next_in():
        sem = rsem.at[len(ins)]
        ins.append(sem)
        return sem

    def take(ref, sem):
        pltpu.make_async_copy(ref, ref, sem).wait()

    def send(src, dst, to, out, into):
        c = pltpu.make_async_remote_copy(
            src_ref=src, dst_ref=dst, send_sem=out, recv_sem=into,
            device_id=to, device_id_type=MESH,
        )
        c.start()
        return c

    loads = [
        (low2.at[:, SK], zb.at[r]),
        (low1, xl.at[x, pl.ds(0, NL)]),
        (piv1, xl.at[x, pl.ds(NL, NM)]),
        (low1, zl.at[r]),
        (low2.at[:, SK], xb.at[x]),
        (g_in, gv),
        (low2.at[:, pl.ds(0, SK)], av),
        (piv2, p2),
    ]
    loads = [pltpu.make_async_copy(a, b, lsem.at[i]) for i, (a, b) in enumerate(loads)]
    for c in loads:
        c.start()
    lane = lax.broadcasted_iota(I32, (8, TC), 1)
    listed = jnp.zeros((8, TC), I32)
    for m in range(NM):
        for p in range(SK):
            listed = jnp.where(lane == m * SK + p, st[m, p], listed)
    sv[y] = listed

    barrier = pltpu.get_barrier_semaphore()
    partners = (x_right, x_left, y_right, y_left, y_far, z_right, z_left, sibling)
    for d in partners:
        pl.semaphore_signal(barrier, inc=1, device_id=d, device_id_type=MESH)
    pl.semaphore_wait(barrier, len(partners))

    class XRing:
        def __init__(self, at, n, half):
            self.at, self.n, self.half = at, n, half

        def both(self, a, b):
            self.into = next_in()
            send(a, a, x_right, self.out, self.into)
            send(b, b, x_left, self.out, self.into)

        def start(self):
            self.out = next_out(self.at(pl.ds(0, 3)))
            self.both(self.at(x), self.at(x))

        def second(self):
            take(self.at(pl.ds(0, 2)), self.into)
            self.both(
                self.at(wrap(x - 1, NX)).at[pl.ds(0, self.half)],
                self.at(wrap(x + 1, NX)).at[pl.ds(self.half, self.n - self.half)],
            )

        def finish(self):
            take(self.at(pl.ds(0, 1)), self.into)

    class ZRing:
        def __init__(self, at, n, half):
            self.at, self.n, self.half = at, n, half

        def both(self, a, b):
            self.into = next_in()
            send(a, a, z_right, self.out, self.into)
            send(b, b, z_left, self.out, self.into)

        def start(self):
            self.out = next_out(self.at(pl.ds(0, 2 * NZ - 1)))
            self.sib = next_in()
            own = self.at(r)
            self.both(own, own)
            send(own, own, sibling, self.out, self.sib)

        def step(self, i):
            take(self.at(pl.ds(0, 2)), self.into)
            a, b = self.at(zrow(z - i)), self.at(zrow(z + i))
            if i < 3:
                self.both(a, b)
            else:
                self.both(
                    a.at[pl.ds(0, self.half)],
                    b.at[pl.ds(self.half, self.n - self.half)],
                )
            send(a, a, sibling, self.out, self.sib)
            send(b, b, sibling, self.out, self.sib)

        def last(self):
            take(self.at(pl.ds(0, 1)), self.into)
            far = self.at(zrow(z + 4))
            send(far, far, sibling, self.out, self.sib)

        def finish(self):
            take(self.at(pl.ds(0, NZ)), self.sib)

    z_b = [
        ZRing(lambda i, m=m: zb.at[i, pl.ds(m * NC, NC)], NC, 1) for m in range(NM)
    ]
    z_l = [
        ZRing(lambda i, m=m: zl.at[i, pl.ds(m * SK, SK)], SK, 2 + m % 2)
        for m in range(NM)
    ]
    z_a = [ZRing(lambda i, j=j: za.at[i, j], SK, 2 + j % 2) for j in range(NJ)]
    x_lp = XRing(lambda i: xl.at[i], NL + NM, (NL + NM) // 2)
    x_b = XRing(lambda i: xb.at[i], NJ, NJ // 2)
    x_a = [XRing(lambda i, m=m: xa.at[i, m], NC * SK, SK) for m in range(NM)]
    x_s = [
        XRing(lambda i, k=k: x3.at[i, k // 2, pl.ds(*UNITS[k % 2])], UNITS[k % 2][1], HALF[k % 2])
        for k in range(2 * NM)
    ]

    listed_in = next_in()

    def send_lists():
        out = next_out(sv.at[pl.ds(0, NY - 1)])
        own = sv.at[y]
        for d in (y_right, y_left, y_far):
            send(own, own, d, out, listed_in)

    def take_lists():
        take(sv.at[pl.ds(0, NY - 1)], listed_in)
        to_scalars = pltpu.make_async_copy(sv, sm, msem)
        to_scalars.start()
        to_scalars.wait()

    def select(delta, k):
        m, (first, count) = k // 2, UNITS[k % 2]
        to = wrap(y + delta, NY)

        def tile_of(e, carry):
            sq = sm[to, 0, m * SK + e // SK]
            sp = sm[to, 0, m * SK + lax.rem(e, SK)]
            mine = sp // NA_LEAF == y
            a = jnp.clip(sp - y * NA_LEAF, 0, NA_LEAF - 1)
            tile = gv[a, sq]
            ysel[delta, m, e] = jnp.where(mine, tile, jnp.zeros_like(tile))
            return carry

        lax.fori_loop(first, first + count, tile_of, 0)

    def halves(k):
        first, count = UNITS[k % 2]
        half = HALF[k % 2]
        return pl.ds(first, half), pl.ds(first + half, count - half)

    y_out = [next_out(ysel.at[pl.ds(0, 3), 0, pl.ds(0, n)]) for _, n in UNITS * NM]
    far_in = [next_in() for _ in range(2 * NM)]
    near_in = [next_in() for _ in range(2 * NM)]

    def y_far_half(k):
        select(2, k)
        m, (lo, hi) = k // 2, halves(k)
        send(ysel.at[2, m, lo], yo.at[m, lo], y_right, y_out[k], far_in[k])
        send(ysel.at[2, m, hi], yo.at[m, hi], y_left, y_out[k], far_in[k])

    def y_near_half(k):
        m, (lo, hi) = k // 2, halves(k)
        select(1, k)
        send(ysel.at[1, m, hi], yn.at[m, 0, hi], y_right, y_out[k], near_in[k])
        select(3, k)
        send(ysel.at[3, m, lo], yn.at[m, 1, lo], y_left, y_out[k], near_in[k])

    def y_merge(k):
        m, (lo, hi) = k // 2, halves(k)
        take(yo.at[m, pl.ds(*UNITS[k % 2])], far_in[k])
        ysel[1, m, lo] = ysel[1, m, lo] + yo[m, lo]
        send(ysel.at[1, m, lo], yn.at[m, 0, lo], y_right, y_out[k], near_in[k])
        ysel[3, m, hi] = ysel[3, m, hi] + yo[m, hi]
        send(ysel.at[3, m, hi], yn.at[m, 1, hi], y_left, y_out[k], near_in[k])

    def y_last(k):
        m, tiles = k // 2, pl.ds(*UNITS[k % 2])
        take(yn.at[m, :, tiles], near_in[k])
        x3[x, m, tiles] = ysel[0, m, tiles] + yn[m, 0, tiles] + yn[m, 1, tiles]
        x_s[k].start()

    def wide(tiles):
        return jnp.concatenate([t.reshape(-1, TC) for t in tiles], axis=1)

    def tall(tiles):
        return tiles.reshape(NR * TR, TC)

    stores = []

    def store(src, dst):
        c = pltpu.make_async_copy(src, dst, osem.at[len(stores)])
        c.start()
        stores.append(c)

    def low_cols(m):
        return wide([xl[i, m * SK : (m + 1) * SK] for i in range(NX)])

    def correct(m):
        lhs = jnp.concatenate(
            [low_cols(m), wide([xl[i, NL + m] for i in range(NX)])], axis=0
        )
        rhs = jnp.concatenate([tall(zb[:, m * NC + c]) for c in range(NC)], axis=1)
        prod = dot3(lhs, rhs, 1)
        for c in range(NC):
            j = m * NC + c
            part = prod[:, c * TC : (c + 1) * TC]
            fixed = av[j] - part[: SK * TR].reshape(SK, TR, TC)
            xa[x, m, c * SK : (c + 1) * SK] = fixed
            za[r, j] = fixed
            pb[j] = part[SK * TR :]

    def spread(j, parts):
        for b, part in enumerate(parts):
            tiles = part.reshape(NZ, 2, TR, TC)
            for hh in range(2):
                gp[hh, j, :, b] = tiles[:, hh]
        reduces[j].share()

    def multiply(m):
        acc = zacc.at[m]
        acc[...] = jnp.zeros(acc.shape, F32)

        def block(q, carry):
            lhs = wide([x3[i, m, pl.ds(q * SK, SK)] for i in range(NX)])
            rhs = jnp.concatenate(
                [tall(zl[:, m * SK + q])]
                + [tall(za[:, m * NC + c, q]) for c in range(NC)],
                axis=1,
            )
            acc[...] += dot3(lhs, rhs, 1)
            return carry

        lax.fori_loop(0, SK, block, 0)
        left = dot3(low_cols(m), acc[...], 0)
        spread(2 * m, [left[:, b * TC : (b + 1) * TC] for b in range(1 + NC)])
        off1[m] = -acc[:, 0:TC].reshape(SK, TR, TC)
        store(off1.at[m], off1_out.at[m])
        upper = pl.ds(0, SK)
        for c in range(NC):
            j = m * NC + c
            off2[j, 0:SK] = -acc[:, (c + 1) * TC : (c + 2) * TC].reshape(SK, TR, TC)
            store(off2.at[j, upper], off2_out.at[j, upper])

    def multiply_own(m):
        parts = []
        for c in range(NC):
            j = m * NC + c
            lhs = jnp.concatenate(
                [
                    wide([xa[i, m, c * SK : (c + 1) * SK] for i in range(NX)]),
                    wide([xb[i, j] for i in range(NX)]),
                ],
                axis=0,
            )
            rhs = jnp.concatenate(
                [zacc[m, :, (c + 1) * TC : (c + 2) * TC], pb[j]], axis=0
            )
            parts.append(dot3(lhs, rhs, 0))
        spread(2 * m + 1, parts)

    class Reduce:
        def __init__(self, j):
            self.j, self.m, self.c = j, j // 2, j % 2
            self.n = 3 - self.c
            self.half = 1 if self.c or self.m % 2 else 2

        def mine(self, zz, a=0, b=None):
            zz = wrap(zz, NZ)
            b = self.n if b is None else b
            return gp[h, self.j, zz, a:b] + sr[self.j, zz, a:b]

        def share(self):
            part = pl.ds(0, self.n)
            out = next_out(gp.at[0, self.j, :, part])
            self.s = send(
                gp.at[1 - h, self.j, :, part],
                sr.at[self.j, :, part],
                sibling,
                out,
                next_in(),
            )

        def both(self, s, right, left):
            j = self.j
            self.into = next_in()
            send(
                send_r.at[j, s, right], in_r.at[j, s, right], z_right, self.out, self.into
            )
            send(send_l.at[j, s, left], in_l.at[j, s, left], z_left, self.out, self.into)

        def arrived(self, pieces):
            take(gp.at[0, self.j, pl.ds(0, pieces), pl.ds(0, self.n)], self.into)

        def start(self):
            j, n, k = self.j, self.n, self.half
            self.out = next_out(gp.at[0, j, pl.ds(0, NZ - 1), pl.ds(0, n)])
            self.s.wait_recv()
            send_r[j, 0, 0:k] = self.mine(z + 4, 0, k)
            send_l[j, 0, k:n] = self.mine(z - 4, k, n)
            self.both(0, pl.ds(0, k), pl.ds(k, n - k))

        def step(self, s):
            j, n, k = self.j, self.n, self.half
            self.arrived(1 if s == 1 else 2)
            if s == 1:
                send_r[j, 1, 0:k] = in_r[j, 0, 0:k] + self.mine(z + 3, 0, k)
                send_r[j, 1, k:n] = self.mine(z + 3, k, n)
                send_l[j, 1, 0:k] = self.mine(z - 3, 0, k)
                send_l[j, 1, k:n] = in_l[j, 0, k:n] + self.mine(z - 3, k, n)
            else:
                send_r[j, s, 0:n] = in_r[j, s - 1, 0:n] + self.mine(z + 4 - s)
                send_l[j, s, 0:n] = in_l[j, s - 1, 0:n] + self.mine(z - 4 + s)
            self.both(s, pl.ds(0, n), pl.ds(0, n))

        def finish(self):
            j, m, c, n = self.j, self.m, self.c, self.n
            self.arrived(2)
            total = in_r[j, 3, 0:n] + in_l[j, 3, 0:n] + self.mine(z)
            if c == 0:
                diag1[m] = xl[x, NL + m] + total[0]
                for i in range(NC):
                    off2[m * NC + i, SK] = total[1 + i] - pb[m * NC + i]
            else:
                for i in range(NC):
                    diag2[m * NC + i] = p2[m * NC + i] + total[i]

    reduces = [Reduce(j) for j in range(2 * NM)]

    for c in loads:
        c.wait()

    send_lists()
    z_b[0].start()
    z_l[0].start()
    z_b[1].start()
    x_lp.start()
    z_l[1].start()
    take_lists()
    y_far_half(0)
    z_b[0].step(1)
    z_b[2].start()
    z_b[1].step(1)
    z_l[0].step(1)
    select(0, 4)
    y_near_half(0)
    x_b.start()
    select(0, 5)
    z_b[2].step(1)
    z_b[0].step(2)
    y_merge(0)
    y_far_half(1)
    x_lp.second()
    z_l[2].start()
    z_b[1].step(2)
    y_near_half(1)
    x_b.second()
    z_b[2].step(2)
    z_b[0].step(3)
    select(0, 0)
    z_l[0].step(2)
    select(0, 1)
    y_last(0)
    z_l[2].step(1)
    select(0, 3)
    z_b[0].last()
    z_b[1].step(3)
    z_l[1].step(1)
    y_merge(1)
    y_far_half(2)
    z_b[0].finish()
    x_lp.finish()
    correct(0)
    z_a[1].start()
    z_a[0].start()
    x_a[0].start()
    z_b[1].last()
    y_near_half(2)
    z_l[0].step(3)
    z_b[2].step(3)
    y_last(1)
    z_l[1].step(2)
    z_b[1].finish()
    correct(1)
    z_a[2].start()
    y_merge(2)
    y_far_half(3)
    z_a[0].step(1)
    select(0, 2)
    x_a[1].start()
    z_b[2].last()
    x_s[0].second()
    z_a[1].step(1)
    z_l[0].last()
    z_a[3].start()
    z_b[2].finish()
    z_a[2].step(1)
    z_l[1].step(3)
    y_near_half(3)
    y_last(2)
    y_merge(3)
    z_a[1].step(2)
    y_far_half(4)
    x_a[1].second()
    z_a[0].step(2)
    z_a[2].step(2)
    correct(2)
    y_near_half(4)
    y_last(3)
    z_a[5].start()
    x_s[2].second()
    z_l[0].finish()
    z_a[4].start()
    x_s[1].second()
    z_a[3].step(1)
    y_merge(4)
    z_a[1].step(3)
    y_far_half(5)
    x_a[0].second()
    y_near_half(5)
    z_a[2].step(3)
    z_a[0].step(3)
    x_b.finish()
    z_a[5].step(1)
    y_last(4)
    z_l[1].last()
    z_a[1].last()
    z_a[3].step(2)
    x_s[2].finish()
    x_s[0].finish()
    z_a[4].step(1)
    y_merge(5)
    z_l[2].step(2)
    z_a[0].last()
    z_a[0].finish()
    z_a[2].last()
    x_s[1].finish()
    z_a[1].finish()
    x_s[3].second()
    z_a[5].step(2)
    x_a[0].finish()
    multiply(0)
    z_a[3].step(3)
    y_last(5)
    x_a[2].start()
    z_l[1].finish()
    reduces[0].start()
    multiply_own(0)
    z_a[4].step(2)
    z_l[2].step(3)
    reduces[1].start()
    x_s[4].second()
    reduces[0].step(1)
    z_a[5].step(3)
    z_a[3].last()
    z_a[3].finish()
    z_a[2].finish()
    x_s[5].second()
    reduces[1].step(1)
    z_a[4].step(3)
    x_s[3].finish()
    multiply(1)
    reduces[0].step(2)
    x_a[2].second()
    z_l[2].last()
    x_a[1].finish()
    multiply_own(1)
    reduces[1].step(2)
    z_a[4].last()
    reduces[2].start()
    reduces[3].start()
    z_l[2].finish()
    z_a[5].last()
    z_a[4].finish()
    reduces[0].step(3)
    z_a[5].finish()
    x_s[4].finish()
    x_s[5].finish()
    multiply(2)
    x_a[2].finish()
    reduces[3].step(1)
    multiply_own(2)
    reduces[4].start()
    reduces[5].start()
    reduces[2].step(1)
    reduces[3].step(2)
    reduces[4].step(1)
    reduces[5].step(1)
    reduces[2].step(2)
    reduces[1].step(3)
    reduces[4].step(2)
    reduces[5].step(2)
    reduces[0].finish()
    reduces[2].step(3)
    reduces[3].step(3)
    reduces[4].step(3)
    reduces[5].step(3)
    reduces[3].finish()
    reduces[1].finish()
    reduces[4].finish()
    reduces[2].finish()
    reduces[5].finish()

    last_row = pl.ds(SK, 1)
    store(off2.at[:, last_row], off2_out.at[:, last_row])
    store(diag1, diag1_out)
    store(diag2, diag2_out)
    for sent, sem in drains:
        take(sent, sem)
    for c in stores:
        c.wait()


def hand_over(*refs):
    n = len(refs) // 2
    for a, b in zip(refs[:n], refs[n:]):
        b[...] = a[...]


def on_device(anc_inverse, struct_one, lower_one, pivot_inv_one, lower_two, pivot_inv_two):
    tile = (TR, TC)

    def vmem(*lead):
        return pltpu.VMEM(lead + tile, F32)

    whole = pl.BlockSpec(memory_space=pltpu.VMEM)
    there = pl.BlockSpec(memory_space=pl.ANY)
    outs = tuple(
        jax.ShapeDtypeStruct(lead + tile, F32)
        for lead in ((NM, SK), (NM,), (NJ, SK + 1), (NJ,))
    )
    made = pl.pallas_call(
        kernel,
        out_shape=outs,
        in_specs=[pl.BlockSpec(memory_space=pltpu.SMEM)] + [there] * 5,
        out_specs=(there,) * 4,
        scratch_shapes=[
            vmem(NM, SK),
            vmem(NM),
            vmem(NJ, SK + 1),
            vmem(NJ),
            vmem(NA_LEAF, NA_ALL),
            vmem(NJ, SK),
            vmem(NJ),
            pltpu.VMEM((NY, 8, TC), I32),
            vmem(NX, NL + NM),
            vmem(NX, NJ),
            vmem(NX, NM, NC * SK),
            vmem(NX, NM, BLK),
            vmem(NR, NJ),
            vmem(NR, NL),
            vmem(NR, NJ, SK),
            vmem(NY, NM, BLK),
            vmem(NM, BLK),
            vmem(NM, 2, BLK),
            pltpu.VMEM((NM, SK * TR, (1 + NC) * TC), F32),
            vmem(NJ),
            vmem(2, NJ, NZ, GT),
            vmem(NJ, NZ, GT),
            vmem(NJ, 4, GT),
            vmem(NJ, 4, GT),
            vmem(NJ, 4, GT),
            vmem(NJ, 4, GT),
            pltpu.SMEM((NY, 8, TC), I32),
            pltpu.SemaphoreType.DMA((N_OUT,)),
            pltpu.SemaphoreType.DMA((N_IN,)),
            pltpu.SemaphoreType.DMA((N_LOADS,)),
            pltpu.SemaphoreType.DMA,
            pltpu.SemaphoreType.DMA((N_STORES,)),
        ],
        compiler_params=pltpu.CompilerParams(
            collective_id=0, has_side_effects=True, vmem_limit_bytes=56 * 2**20
        ),
    )(
        struct_one,
        anc_inverse,
        lower_one.reshape(NL, TR, TC),
        pivot_inv_one,
        lower_two,
        pivot_inv_two,
    )
    return pl.pallas_call(
        hand_over,
        out_shape=outs,
        in_specs=[whole] * 4,
        out_specs=(whole,) * 4,
    )(*made)


def solution(mesh):
    placed = (
        P("leaf", None, "row", "col"),
        P("leaf", None),
        P("leaf", None, "row", "col"),
        P("leaf", "row", "col"),
        P("leaf", None, "row", "col"),
        P("leaf", "row", "col"),
    )
    return jax.shard_map(
        on_device,
        mesh=mesh,
        in_specs=placed,
        out_specs=(
            P("leaf", None, "row", "col"),
            P("leaf", "row", "col"),
            P("leaf", None, "row", "col"),
            P("leaf", "row", "col"),
        ),
        check_vma=False,
    )
```
